32 devices in a mesh: gx: 8 (over z, core), gy: 4 (over y, x).
Axes of the slice: x: 2, y: 2, z: 4, core: 2. Of those that a mesh axis runs over, the one named last changes fastest.
Arguments:
- p_prev: float32 [48, 1024, 512], P(None, 'gx', 'gy'), may hold values from -6 to 6
- p_cur: float32 [48, 1024, 512], P(None, 'gx', 'gy'), may hold values from -6 to 6
- courant: float32 [48, 1024, 512], P(None, 'gx', 'gy'), may hold values from 0.04 to 0.2
- snapshots: bfloat16 [3, 48, 1024, 512], P(None, None, 'gx', 'gy'), may hold values from -6 to 6
- residual: float32 [4, 65536, 128], P(None, ('gx', 'gy')), may hold values from -6 to 6
- rec_owner: int32 [65536, 1], P(('gx', 'gy')), may hold values from 0 to 31; in each aligned block of 2048 rows (0 to 2047, 2048 to 4095, ...) at most 128 rows name the same one
- rec_cell: int32 [65536], P(('gx', 'gy')), may hold values from 0 to 16383
- signs: int32 [4], replicated, may hold values from -1 to 1, as said below
Outputs:
- adjoint_field: float32 [48, 1024, 512], P(None, 'gx', 'gy')
- image: float32 [48, 1024, 512], P(None, 'gx', 'gy')
The draws below stay inside these ranges and needn't reach their ends.
Inputs may be any that keep to these rules, and one draw needn't show every extreme that they name: `rec_owner`: in the rows of one device no owner is named more than 128 times, a bound that some block reaches. `signs`: each entry is +1 or -1, and both occur.
All inputs are finite; a program needn't handle non-finite values.
Results may differ from the reference program's by a relative error of at most 0.0003.
Values sent between devices are 32-bit elements; how exact they have to be, the bound alone decides.
A program may use at most 128 MiB of HBM per device.

```python
import math
import jax
import jax.numpy as jnp
import numpy as np
from jax import lax

NZ = 48
CX = 128
CY = 128
STEPS = 3
SHOTS = 4
NT = 128
RECV_DEPTH = 2
RECV_DEV = 2048
CAP = 128
NX = 1024
NY = 512
RECV = 65536
N_GY = 4
DEVICES = 32


def draw_signs(key, part):
    order = jax.random.permutation(key, jnp.arange(SHOTS))
    return (2 * (order % 2) - 1).astype(jnp.int32)


def plant(result, stream_key, low, high):
    dims = result.shape
    place = [jax.random.randint(jax.random.fold_in(stream_key, axis), (), 0, dims[axis]) for axis in range(len(dims))]
    result = result.at[tuple(place)].set(low)
    longest = dims.index(max(dims))
    place[longest] = (place[longest] + 1) % dims[longest]
    return result.at[tuple(place)].set(high)


def steps_of(key, extent, pieces, smallest, top_value):
    level = 1.0
    for position, blocks in pieces:
        heights = jax.random.uniform(jax.random.fold_in(jax.random.fold_in(key, 6), position), (blocks,), jnp.float32, smallest / len(pieces), top_value / len(pieces))
        level = level * jnp.repeat(jnp.exp(heights), extent[position] // blocks).reshape((-1,) + (1,) * (len(extent) - 1 - position))
    return level


def deal_out(key, own, number, rows, count, top, most, slope):
    order = jax.random.permutation(key, count)
    heavy_load, usual = load_shares(count, rows * top, most, slope, True), load_shares(count, rows * top, most, slope, False)
    places = jnp.arange(count)

    def named(sizes, offset_by):
        used = int((sizes > 0).sum())
        fixed = max(1, used // 4)
        passed = fixed + (places - fixed + offset_by * (used - fixed)) % max(1, count - fixed)
        return jnp.zeros((count,), jnp.int32).at[order[jnp.where(places < fixed, places, passed)]].set(jnp.asarray(sizes, jnp.int32))

    sizes = jnp.where(number % 4 == 0, named(heavy_load, number // 4), named(usual, number - number // 4 - 1))
    mixed = jax.random.permutation(jax.random.fold_in(own, 3), count)
    giver, receiver = mixed[0:count // 2 * 2:2], mixed[1:count // 2 * 2:2]
    room = jnp.minimum(sizes[giver] - 1, most - sizes[receiver]) // 2
    room = jnp.where((giver == order[0]) | (receiver == order[0]) | (sizes[receiver] == 0), 0, jnp.maximum(room, 0))
    passed = jax.random.randint(jax.random.fold_in(own, 4), (count // 2,), 0, 1 << 20) % (room + 1)
    sizes = sizes.at[giver].add(-passed).at[receiver].add(passed)
    labels = jnp.searchsorted(jnp.cumsum(sizes), jnp.arange(rows * top), side="right").astype(jnp.int32)
    listing = labels.reshape(top, rows).T
    listing = listing[jax.random.permutation(jax.random.fold_in(own, 1), rows)]
    offset_by = jax.random.randint(jax.random.fold_in(own, 2), (rows, 1), 0, top)
    return jnp.take_along_axis(listing, (jnp.arange(top)[None, :] + offset_by) % top, axis=1)


def load_shares(number_of, total, bound, skew, full):
    portions = [(1 << 20) // math.isqrt(rank ** skew) + 1 for rank in range(1, number_of + 1)]
    largest = bound if full else min(bound, max(-(-total // number_of), total * portions[0] // sum(portions)))
    least = 1 if total - largest >= number_of - 1 else 0
    holding, surplus = [largest] + [least] * (number_of - 1), total - largest - least * (number_of - 1)
    while surplus > 0:
        movable = [i for i in range(1, number_of) if holding[i] < largest] or [i for i in range(1, number_of) if holding[i] < bound]
        mass, left = sum([portions[i] for i in movable]), surplus
        for i in movable:
            more = min(bound - holding[i], max(1, left * portions[i] // mass), surplus)
            holding[i] = holding[i] + more
            surplus = surplus - more
    return np.array(holding)


def scatter_about(key, extent, scale, limit, shards=(), dtype=jnp.bfloat16):
    values = jax.random.normal(key, extent, jnp.float32) * scale
    if len(shards) > 0:
        values = steps_of(key, extent, shards, -0.22, 0.18) * values
    return jnp.clip(values, min=-limit, max=limit).astype(dtype)


def setup_inputs(seed: int = 0) -> dict:
    key_of = jax.random.split(jax.random.key(seed), 9)
    p_prev = scatter_about(key_of[0], (NZ, NX, NY), 1.0, 6.0, ((1, 8), (2, 4)), jnp.float32)
    p_cur = scatter_about(key_of[1], (NZ, NX, NY), 1.0, 6.0, ((1, 8), (2, 4)), jnp.float32)
    courant = jnp.clip(jnp.exp(math.log(0.2) - 1.609438 * jax.random.uniform(key_of[2], (NZ, NX, NY), jnp.float32) ** steps_of(key_of[2], (NZ, NX, NY), ((1, 8), (2, 4)), -0.2, 0.2)), 0.04, 0.2)
    snapshots = scatter_about(key_of[3], (STEPS, NZ, NX, NY), 1.0, 6.0, ((2, 8), (3, 4)))
    residual = scatter_about(key_of[4], (SHOTS, RECV, NT), 1.0, 6.0, ((1, 32),), jnp.float32)
    rec_owner_keys = jax.random.split(jax.random.fold_in(key_of[5], 1), RECV // RECV_DEV)
    rec_owner_turns = jax.random.permutation(jax.random.fold_in(key_of[5], 3), RECV // RECV_DEV)
    rec_owner = jax.vmap(lambda own, number: deal_out(jax.random.fold_in(key_of[5], 2), own, number, RECV_DEV, DEVICES, 1, CAP, 2))(rec_owner_keys, rec_owner_turns).reshape((RECV, 1))
    rec_cell = plant(jax.random.randint(key_of[6], (RECV,), 0, CX * CY), jax.random.fold_in(key_of[6], 1), 0, (CX * CY) - 1).astype(jnp.int32)
    signs = draw_signs(jax.random.fold_in(key_of[8], 71), 0)
    return {"p_prev": p_prev, "p_cur": p_cur, "courant": courant, "snapshots": snapshots, "residual": residual, "rec_owner": rec_owner, "rec_cell": rec_cell, "signs": signs}


COEFF = (-205.0 / 72.0, 8.0 / 5.0, -1.0 / 5.0, 8.0 / 315.0, -1.0 / 560.0)

def laplace(ext):
    depth = ext.shape[0]
    width_a = ext.shape[1] - 8
    width_b = ext.shape[2] - 8
    center = ext[:, 4:4 + width_a, 4:4 + width_b]
    zpad = jnp.pad(center, ((4, 4), (0, 0), (0, 0)))
    total = 3.0 * COEFF[0] * center
    for i in range(1, 5):
        near = ext[:, 4 + i:4 + i + width_a, 4:4 + width_b] + ext[:, 4 - i:4 - i + width_a, 4:4 + width_b]
        near = near + ext[:, 4:4 + width_a, 4 + i:4 + i + width_b] + ext[:, 4:4 + width_a, 4 - i:4 - i + width_b]
        near = near + zpad[4 + i:4 + i + depth] + zpad[4 - i:4 - i + depth]
        total = total + COEFF[i] * near
    return total

def step_table(samples, steps):
    rows = jnp.arange(samples).astype(jnp.float32)[:, None]
    cols = jnp.arange(steps).astype(jnp.float32)[None, :]
    return jnp.cos(math.pi * (cols + 0.5) * (rows + 0.5) / samples) * math.sqrt(2.0 / samples)

def reference(p_prev, p_cur, courant, snapshots, residual, rec_owner, rec_cell, signs):
    encoded = lax.optimization_barrier(jnp.sum(signs.astype(jnp.float32)[:, None, None] * residual, axis=0))
    amps = jnp.dot(encoded, step_table(NT, STEPS), precision=lax.Precision.HIGHEST)
    owner = rec_owner[:, 0]
    inline = owner // N_GY * CX + rec_cell // CY
    cross = owner % N_GY * CY + rec_cell % CY
    injection = jnp.zeros((STEPS, NX, NY), jnp.float32).at[:, inline, cross].add(amps.T)
    prev, cur = (p_prev, p_cur)
    image = jnp.zeros(p_cur.shape, jnp.float32)
    for k in range(STEPS):
        ext = jnp.pad(cur, ((0, 0), (4, 4), (4, 4)))
        nxt = 2.0 * cur - prev + courant * laplace(ext)
        nxt = nxt.at[RECV_DEPTH].add(courant[RECV_DEPTH] * injection[k])
        image = image + snapshots[k].astype(jnp.float32) * nxt
        prev, cur = (cur, nxt)
    return (cur, image)
```

```python
import functools
import math

import jax
import jax.numpy as jnp
import numpy as np
from jax import lax
from jax.experimental import pallas as pl
from jax.experimental.pallas import tpu as pltpu
from jax.sharding import PartitionSpec as P

STEPS = 3
NT = 128
RECV_DEPTH = 2
HALO = 4
CHUNK = 16
BLOCK = 256
GROUP = 8
SENDERS = 8

SCALE = 5040.0
CENTER_Y, CENTER_X = -43008.0, -42.0
TAPS = (8064.0, -1008.0, 128.0, -9.0)

F32 = jnp.float32
BF16 = jnp.bfloat16
I32 = jnp.int32
MESH = pl.DeviceIdType.MESH


def taps(distance):
    out = jnp.zeros(distance.shape, F32)
    for i, c in enumerate(TAPS):
        out = jnp.where(distance == i + 1, c, out)
    return out


def pieces(v):
    hi = v.astype(BF16)
    return hi, (v - hi.astype(F32)).astype(BF16)


def iota(shape, dim):
    return lax.broadcasted_iota(I32, shape, dim)


def lanes_dot(a, b, **kw):
    return lax.dot_general(a, b, (((1,), (1,)), ((), ())), preferred_element_type=F32, **kw)


def side_taps(nx):
    row = iota((16, 16), 0)
    src = iota((16, 16), 1) & 7
    place = jnp.where(src < 4, src - 4, nx + src - 4)
    target = jnp.where(row < 8, row, nx - 16 + row)
    return taps(jnp.abs(place - target)).astype(BF16)


def border_of(h_x, overs):
    cols = []
    for over in overs:
        hi, lo = pieces(over)
        cols.append(jnp.concatenate([hi.astype(F32), lo.astype(F32)], axis=0).astype(BF16))
    return jnp.dot(h_x, jnp.concatenate(cols, axis=1), preferred_element_type=F32)


def lateral(t_x, t_y, vs):
    (hi0, lo0), (hi1, lo1) = pieces(vs[0]), pieces(vs[1])
    hi = jnp.concatenate([hi0, hi1], axis=1)
    lo = jnp.concatenate([lo0, lo1], axis=1)
    return jnp.dot(
        jnp.concatenate([hi, lo, t_x[...]], axis=1),
        jnp.concatenate([t_y[...], t_y[...], hi, lo], axis=0),
        preferred_element_type=F32,
    )


def deep(cur, at):
    depth = TAPS[0] * (cur[at + 1] + cur[at - 1])
    for r in range(2, HALO + 1):
        depth = depth + TAPS[r - 1] * (cur[at + r] + cur[at - r])
    return depth


def with_border(lap, border):
    nx = lap.shape[0]
    return jnp.concatenate([lap[:8] + border[:8], lap[8 : nx - 8], lap[nx - 8 :] + border[8:]], axis=0)


def gather_edges(vs):
    lane = iota(vs[0].shape, 1)
    width = 1
    while len(vs) > 1:
        inside = (lane >= 8 * width - 4) & (lane < 16 * width - 4)
        vs = [
            jnp.where(inside, pltpu.roll(b, 8 * width, 1), a) for a, b in zip(vs[::2], vs[1::2])
        ]
        width *= 2
    return vs[0]


def to_sides(first, second):
    nx, ny = first.shape
    half = nx // 2
    lane = iota((nx, ny), 1)
    whole = jnp.where((lane >= ny // 2 - 4) & (lane < ny - 4), pltpu.roll(second, ny // 2, 1), first)
    top, low = whole[:half], pltpu.roll(whole[half:], 4, 1)
    odd = (iota((half, ny), 1) & 4) != 0
    return jnp.where(odd, top, low), jnp.where(odd, low, top)


def edge_terms(left, right, onto):
    half, ny = left.shape
    odd = (iota((half, ny), 1) & 4) != 0
    edges = jnp.concatenate(
        [jnp.where(odd, left, right), pltpu.roll(jnp.where(odd, right, left), ny - 4, 1)], axis=0
    )
    return jnp.dot(
        jnp.concatenate(pieces(edges), axis=1), jnp.concatenate([onto[...]] * 2, axis=0),
        preferred_element_type=F32,
    )


def placed_edge(terms, q):
    nx, ny = terms.shape
    lane = iota((nx, ny), 1)
    turned = pltpu.roll(terms, (2 * ny - 4 - 8 * q) & (ny - 1), 1)
    return jnp.where((lane < HALO) | (lane >= ny - HALO), turned, 0.0)


def main_kernel(
    n_gx, n_gy, signs, owner_h, cell_h, table_h, t_x_h, t_y_h, onto_h,
    p_prev, p_cur, courant_h, snaps_h, residual_h,
    buf_a, buf_b, courant, snaps, image, edge_out, over_out, source_out,
    owner, cell, table, t_x, t_y, onto, residual, sx, rx, sy, ry, edge, planes, packed,
    snd, got, load_sem, sxs, rxs, sys_, rys, snds, gots,
):
    n = n_gx * n_gy
    nz, nx, ny = p_cur.shape
    half, mid = nx // 2, ny // 2
    chunks = nz // CHUNK
    deeper = tuple(range(chunks - 1, 0, -1))
    gx, gy = lax.axis_index("gx"), lax.axis_index("gy")
    me = gx * n_gy + gy

    inner = pl.ds(HALO, nz)
    plan = [
        (p_cur, buf_a.at[inner]), (residual_h, residual), (owner_h, owner), (cell_h, cell), (table_h, table),
        (t_x_h, t_x), (t_y_h, t_y), (p_prev, buf_b.at[inner]), (courant_h, courant), (onto_h, onto),
        (snaps_h, snaps),
    ]
    loads = [pltpu.make_async_copy(s, d, load_sem.at[i]) for i, (s, d) in enumerate(plan)]
    for load in loads:
        load.start()

    barrier = pltpu.get_barrier_semaphore()

    def greet(o, carry):
        d = lax.rem(me + o, n)
        pl.semaphore_signal(
            barrier, inc=1, device_id=(d // n_gy, lax.rem(d, n_gy)), device_id_type=MESH
        )
        return carry

    lax.fori_loop(1, n, greet, 0)

    h_x = side_taps(nx)
    zero = jnp.zeros((HALO, nx, ny), F32)
    for buf in (buf_a, buf_b):
        buf[pl.ds(0, HALO)] = zero
        buf[pl.ds(HALO + nz, HALO)] = zero

    for side, absent in ((0, gx == 0), (1, gx == n_gx - 1)):

        @pl.when(absent)
        def _(side=side):
            for k in range(STEPS):
                rx[k, side] = jnp.zeros(rx.shape[2:], F32)

    for side, absent in ((0, gy == 0), (1, gy == n_gy - 1)):

        @pl.when(absent)
        def _(side=side):
            for k in range(STEPS):
                ry[k, side] = jnp.zeros(ry.shape[2:], F32)

    def pack(vs, k, g, j):
        for i, v in enumerate(vs):
            z = g * CHUNK + GROUP * j + i
            sx[k, 0, z] = v[nx - HALO :]
            sx[k, 1, z] = v[:HALO]
        packed[k % 2, j] = gather_edges(vs)

    def settle(k, g):
        sy[k, 0, g], sy[k, 1, g] = to_sides(packed[k % 2, 0], packed[k % 2, 1])

    def halo_copies(k, g):
        zs = pl.ds(g * CHUNK, CHUNK)
        out = []
        for side, step, send_ok, recv_ok in (
            (0, 1, gx < n_gx - 1, gx > 0),
            (1, -1, gx > 0, gx < n_gx - 1),
        ):
            i = (k * chunks + g) * 2 + side
            copy = pltpu.make_async_remote_copy(
                src_ref=sx.at[k, side, zs], dst_ref=rx.at[k, side, zs],
                send_sem=sxs.at[i], recv_sem=rxs.at[i],
                device_id=(lax.rem(gx + step + n_gx, n_gx), gy), device_id_type=MESH,
            )
            out.append((copy, send_ok, recv_ok))
        for side, step, send_ok, recv_ok in (
            (0, 1, gy < n_gy - 1, gy > 0),
            (1, -1, gy > 0, gy < n_gy - 1),
        ):
            i = (k * chunks + g) * 2 + side
            copy = pltpu.make_async_remote_copy(
                src_ref=sy.at[k, side, g], dst_ref=ry.at[k, side, g],
                send_sem=sys_.at[i], recv_sem=rys.at[i],
                device_id=(gx, lax.rem(gy + step + n_gy, n_gy)), device_id_type=MESH,
            )
            out.append((copy, send_ok, recv_ok))
        return out

    def send_halo(k, g):
        for copy, send_ok, _ in halo_copies(k, g):
            pl.when(send_ok)(copy.start)

    def wait_halo(k, g):
        for copy, _, recv_ok in halo_copies(k, g):
            pl.when(recv_ok)(copy.wait_recv)

    def each(body):
        lax.fori_loop(0, CHUNK // GROUP, lambda j, c: (body(j), c)[1], 0)

    def beyond(k, z):
        return jnp.concatenate([rx[k, 0, z], rx[k, 1, z]], axis=0)

    loads[0].wait()
    for g in range(chunks):

        def first_pack(j, g=g):
            pack([buf_a[HALO + g * CHUNK + GROUP * j + i] for i in range(GROUP)], 0, g, j)

        each(first_pack)
        settle(0, g)

    for load in loads[1:5]:
        load.wait()
    recv_dev = owner.shape[1]
    slots = snd.shape[2]
    upper = (iota((BLOCK, BLOCK), 0) < iota((BLOCK, BLOCK), 1)).astype(F32).astype(BF16)
    count = jnp.zeros((n, 1), F32)
    message = jnp.zeros((n * 8, slots), F32)
    part = iota((8, BLOCK), 0)
    shift = ny.bit_length() - 1
    for blk in range(recv_dev // BLOCK):
        rows = pl.ds(blk * BLOCK, BLOCK)
        enc = signs[0].astype(F32) * residual[0, rows, :]
        for s in range(1, residual.shape[0]):
            enc = enc + signs[s].astype(F32) * residual[s, rows, :]
        both = lanes_dot(table[...], jnp.concatenate(pieces(enc), axis=1))
        amps = both[:8] + both[8:]
        hi = amps.astype(BF16).astype(F32)
        c = cell[:, rows]
        at_x = (c >> shift).astype(F32)
        at_y = (c & (ny - 1)).astype(F32)
        payload = jnp.where((part & 1) == 0, hi, amps - hi)
        payload = jnp.where(part == 6, at_x, payload)
        payload = jnp.where(part == 7, at_y, payload)
        onehot = jnp.where(iota((n, BLOCK), 0) == owner[:, rows], 1.0, 0.0)
        before = jnp.dot(onehot.astype(BF16), upper, preferred_element_type=F32) + count
        count = count + jnp.sum(onehot, axis=1, keepdims=True)
        rank = jnp.sum(before * onehot, axis=0, keepdims=True)
        spread = (onehot[:, None, :] * payload[None]).reshape(n * 8, BLOCK).astype(BF16)
        slot = jnp.where(iota((slots, BLOCK), 0).astype(F32) == rank, 1.0, 0.0).astype(BF16)
        message = message + lanes_dot(spread, slot)
    snd[...] = message.reshape(n, 8, slots)
    got[me] = snd[me]

    def message_to(o):
        d = lax.rem(me + o, n)
        return pltpu.make_async_remote_copy(
            src_ref=snd.at[d], dst_ref=got.at[me], send_sem=snds.at[o], recv_sem=gots.at[o],
            device_id=(d // n_gy, lax.rem(d, n_gy)), device_id_type=MESH,
        )

    def post(o, carry):
        message_to(o).start()
        return carry

    def step_chunk(k, g, inside=False):
        cur, prev = (buf_a, buf_b) if k % 2 == 0 else (buf_b, buf_a)
        if not inside:
            wait_halo(k, g)
            edge[...] = edge_terms(ry[k, 0, g], ry[k, 1, g], onto)

        def body(j):
            qs = [GROUP * j + i for i in range(GROUP)]
            made = []
            for p in range(GROUP // 2):
                pair = qs[2 * p : 2 * p + 2]
                zs = [g * CHUNK + q for q in pair]
                vs = [cur[z + HALO] for z in zs]
                lap2 = lateral(t_x, t_y, vs)
                border2 = None if inside else border_of(h_x, [beyond(k, z) for z in zs])
                for i, (z, v) in enumerate(zip(zs, vs)):
                    cols = slice(i * ny, (i + 1) * ny)
                    lap = lap2[:, cols] + deep(cur, z + HALO)
                    if not inside:
                        lap = with_border(lap + placed_edge(edge[...], pair[i]), border2[:, cols])
                    if k == 0:
                        speed = courant[z] * (1.0 / SCALE)
                        courant[z] = speed
                    else:
                        speed = courant[z]
                    old = prev[z + HALO]
                    nxt = (2.0 * v - old) + speed * lap
                    if k == STEPS - 1:
                        image[z] = (
                            snaps[0, z].astype(F32) * old + snaps[1, z].astype(F32) * v
                            + snaps[2, z].astype(F32) * nxt
                        )
                    prev[z + HALO] = nxt
                    made.append(nxt)
            if k < STEPS - 1 and not inside:
                pack(made, k + 1, g, j)

        each(body)
        if k < STEPS - 1 and not inside and (k, g) != (0, 0):
            settle(k + 1, g)

    def complete(g):
        wait_halo(0, g)
        edge[...] = edge_terms(ry[0, 0, g], ry[0, 1, g], onto)

        def body(j):
            qs = [GROUP * j + i for i in range(GROUP)]
            made = []
            for p in range(GROUP // 2):
                zs = [g * CHUNK + q for q in qs[2 * p : 2 * p + 2]]
                border2 = border_of(h_x, [beyond(0, z) for z in zs])
                for i, z in enumerate(zs):
                    cols = slice(i * ny, (i + 1) * ny)
                    lap = with_border(placed_edge(edge[...], qs[2 * p + i]), border2[:, cols])
                    nxt = buf_b[z + HALO] + courant[z] * lap
                    buf_b[z + HALO] = nxt
                    made.append(nxt)
            pack(made, 1, g, j)

        each(body)
        settle(1, g)
        send_halo(1, g)

    for load in loads[5:9]:
        load.wait()
    step_chunk(0, deeper[0], inside=True)
    pl.semaphore_wait(barrier, n - 1)
    for g in deeper + (0,):
        send_halo(0, g)
    lax.fori_loop(1, n, post, 0)
    for g in deeper[1:]:
        step_chunk(0, g, inside=True)
    loads[9].wait()
    for g in deeper:
        complete(g)
    step_chunk(0, 0)
    for g in deeper:
        step_chunk(1, g)
        send_halo(2, g)

    def arrive(o, carry):
        d = lax.rem(me - o + n, n)
        pltpu.make_async_remote_copy(
            src_ref=snd.at[d], dst_ref=got.at[d], send_sem=snds.at[o], recv_sem=gots.at[o],
            device_id=(d // n_gy, lax.rem(d, n_gy)), device_id_type=MESH,
        ).wait_recv()
        return carry

    lax.fori_loop(1, n, arrive, 0)
    planes[...] = jnp.zeros(planes.shape, F32)
    row_x = iota((nx, slots), 0).astype(F32)
    row_y = iota((ny, slots), 0).astype(F32)

    def gather(j, carry):
        lhs, rhs = [], [[] for _ in range(2 * STEPS)]
        for i in range(SENDERS):
            block = got[SENDERS * j + i]
            lhs.append(jnp.where(row_x == block[6:7], 1.0, 0.0).astype(BF16))
            at_y = row_y == block[7:8]
            for h in range(2 * STEPS):
                rhs[h].append(jnp.where(at_y, block[h : h + 1], 0.0).astype(BF16))
        rhs = jnp.concatenate([jnp.concatenate(r, axis=1) for r in rhs], axis=0)
        planes[...] += lanes_dot(jnp.concatenate(lhs, axis=1), rhs)
        return carry

    lax.fori_loop(0, n // SENDERS, gather, 0)

    def source(k):
        cols = planes[:, 2 * k * ny : (2 * k + 2) * ny]
        return (SCALE * courant[RECV_DEPTH]) * (cols[:, :ny] + cols[:, ny:])

    at = HALO + RECV_DEPTH
    fixed = buf_b[at] + source(0)
    buf_b[at] = fixed
    sx[1, 0, RECV_DEPTH] = fixed[nx - HALO :]
    sx[1, 1, RECV_DEPTH] = fixed[:HALO]
    near = 8 * RECV_DEPTH - 4
    lane = iota((nx, ny), 1)
    packed[1, 0] = jnp.where(
        (lane >= near) & (lane < near + 8), pltpu.roll(fixed, 8 * RECV_DEPTH, 1), packed[1, 0]
    )
    settle(1, 0)
    send_halo(1, 0)
    loads[10].wait()
    step_chunk(2, deeper[0])
    buf_a[at] = buf_a[at] - source(1)
    step_chunk(1, 0)
    send_halo(2, 0)
    for g in deeper[1:]:
        step_chunk(2, g)
    source_out[...] = source(2)
    wait_halo(2, 0)
    edge_out[...] = edge_terms(ry[2, 0, 0], ry[2, 1, 0], onto)
    over_out[:, :HALO] = rx[2, 0, pl.ds(0, CHUNK)]
    over_out[:, HALO:] = rx[2, 1, pl.ds(0, CHUNK)]

    def finish(o, carry):
        message_to(o).wait_send()
        return carry

    lax.fori_loop(1, n, finish, 0)
    for k in range(STEPS):
        for g in range(chunks):
            for copy, send_ok, _ in halo_copies(k, g):
                pl.when(send_ok)(copy.wait_send)


def last_kernel(
    buf_a, buf_b, courant, snaps, image, edge, over, source, t_x_h, t_y_h,
    field_out, image_out,
    t_x, t_y, field0, image0, load_sem, out_sem,
):
    nz, nx, ny = courant.shape
    chunks = nz // CHUNK
    loads = [
        pltpu.make_async_copy(s, d, load_sem.at[i])
        for i, (s, d) in enumerate(((t_x_h, t_x), (t_y_h, t_y)))
    ]
    for load in loads:
        load.start()
    outs = []
    for g in range(chunks - 1, 0, -1):
        zs = pl.ds(g * CHUNK, CHUNK)
        outs += [
            pltpu.make_async_copy(
                buf_b.at[pl.ds(HALO + g * CHUNK, CHUNK)], field_out.at[zs], out_sem.at[2 * g]
            ),
            pltpu.make_async_copy(image.at[zs], image_out.at[zs], out_sem.at[2 * g + 1]),
        ]
    for out in outs:
        out.start()
    h_x = side_taps(nx)
    for load in loads:
        load.wait()

    def rest(j):
        zs = pl.ds(j * GROUP, GROUP)
        return [
            pltpu.make_async_copy(field0.at[zs], field_out.at[zs], out_sem.at[2 * chunks + 2 * j]),
            pltpu.make_async_copy(image0.at[zs], image_out.at[zs], out_sem.at[2 * chunks + 2 * j + 1]),
        ]

    def body(j, carry):
        for p in range(GROUP // 2):
            zs = [GROUP * j + 2 * p + i for i in range(2)]
            vs = [buf_a[z + HALO] for z in zs]
            lap2 = lateral(t_x, t_y, vs)
            border2 = border_of(h_x, [over[z] for z in zs])
            for i, (z, v) in enumerate(zip(zs, vs)):
                cols = slice(i * ny, (i + 1) * ny)
                lap = lap2[:, cols] + deep(buf_a, z + HALO) + placed_edge(edge[...], z)
                lap = with_border(lap, border2[:, cols])
                old = buf_b[z + HALO]
                nxt = (2.0 * v - old) + courant[z] * lap
                nxt = nxt + jnp.where(z == RECV_DEPTH, source[...], 0.0)
                field0[z] = nxt
                image0[z] = (
                    snaps[0, z].astype(F32) * old + snaps[1, z].astype(F32) * v
                    + snaps[2, z].astype(F32) * nxt
                )
        for out in rest(j):
            out.start()
        return carry

    lax.fori_loop(0, CHUNK // GROUP, body, 0)
    for j in range(CHUNK // GROUP):
        for out in rest(j):
            out.wait()
    for out in outs:
        out.wait()


def step_table(samples, steps):
    rows = np.arange(samples, dtype=np.float64)[None, :]
    cols = np.repeat(np.arange(steps, dtype=np.float64), 2)[:, None]
    table = np.cos(math.pi * (cols + 0.5) * (rows + 0.5) / samples) * math.sqrt(2.0 / samples)
    table = np.concatenate([table, np.zeros((8 - 2 * steps, samples))]).astype(np.float32)
    hi = table.astype(jnp.bfloat16)
    lo = (table - hi.astype(np.float32)).astype(jnp.bfloat16)
    return np.concatenate(
        [np.concatenate([hi, hi], axis=1), np.concatenate([lo, np.zeros_like(lo)], axis=1)], axis=0
    )


def tap_values(distance):
    out = np.zeros(distance.shape, np.float32)
    for i, c in enumerate(TAPS):
        out[distance == i + 1] = c
    return out


def band(size, center):
    a = np.arange(size)
    distance = np.abs(a[:, None] - a[None, :])
    return np.where(distance == 0, np.float32(center), tap_values(distance))


def matrices(nx, ny):
    t_x = np.concatenate([band(nx, CENTER_X)] * 2, axis=1)
    t_y = np.zeros((2 * ny, 2 * ny), np.float32)
    t_y[:ny, :ny] = t_y[ny:, ny:] = band(ny, CENTER_Y)
    a, b = np.arange(ny)[:, None], np.arange(ny)[None, :]
    left = (a & 4) != 0
    place = np.where(left, (a & 3) - 4, ny + (a & 3))
    plane = np.where(left, (a + 4) % ny, a) >> 3
    target = np.where((b & 7) < 4, ny - 4 + (b & 7), (b & 7) - 4)
    onto = np.where(plane == b >> 3, tap_values(np.abs(place - target)), np.float32(0))
    return [jnp.asarray(m.astype(jnp.bfloat16)) for m in (t_x, t_y, onto)]


def shards(n_gx, n_gy, p_prev, p_cur, courant, snapshots, residual, rec_owner, rec_cell, signs):
    nz, nx, ny = p_cur.shape
    n = n_gx * n_gy
    recv_dev = rec_cell.shape[0]
    slots = -(-(2 * recv_dev // n) // 128) * 128
    chunks = nz // CHUNK
    anywhere = pl.BlockSpec(memory_space=pl.ANY)
    vmem = pl.BlockSpec(memory_space=pltpu.VMEM)
    dma = pltpu.SemaphoreType.DMA
    whole = jax.ShapeDtypeStruct(p_cur.shape, F32)
    mats = matrices(nx, ny)
    mat_scratch = [pltpu.VMEM(m.shape, BF16) for m in mats]
    table = jnp.asarray(step_table(NT, STEPS))
    state = (
        pltpu.VMEM((nz + 2 * HALO, nx, ny), F32),
        pltpu.VMEM((nz + 2 * HALO, nx, ny), F32),
        pltpu.VMEM((nz, nx, ny), F32),
        pltpu.VMEM((STEPS, nz, nx, ny), BF16),
        pltpu.VMEM((nz, nx, ny), F32),
        pltpu.VMEM((nx, ny), F32),
        pltpu.VMEM((CHUNK, 2 * HALO, ny), F32),
        pltpu.VMEM((nx, ny), F32),
    )
    held = pl.pallas_call(
        functools.partial(main_kernel, n_gx, n_gy),
        out_shape=state,
        in_specs=[pl.BlockSpec(memory_space=pltpu.SMEM)] + [anywhere] * 11,
        out_specs=(vmem,) * len(state),
        scratch_shapes=[
            pltpu.VMEM((1, recv_dev), I32),
            pltpu.VMEM((1, recv_dev), I32),
            pltpu.VMEM(table.shape, BF16),
            *mat_scratch,
            pltpu.VMEM(residual.shape, F32),
            pltpu.VMEM((STEPS, 2, nz, HALO, ny), F32),
            pltpu.VMEM((STEPS, 2, nz, HALO, ny), F32),
            pltpu.VMEM((STEPS, 2, chunks, nx // 2, ny), F32),
            pltpu.VMEM((STEPS, 2, chunks, nx // 2, ny), F32),
            pltpu.VMEM((nx, ny), F32),
            pltpu.VMEM((nx, 2 * STEPS * ny), F32),
            pltpu.VMEM((2, CHUNK // GROUP, nx, ny), F32),
            pltpu.VMEM((n, 8, slots), F32),
            pltpu.VMEM((n, 8, slots), F32),
            dma((11,)),
            dma((2 * STEPS * chunks,)),
            dma((2 * STEPS * chunks,)),
            dma((2 * STEPS * chunks,)),
            dma((2 * STEPS * chunks,)),
            dma((n,)),
            dma((n,)),
        ],
        compiler_params=pltpu.CompilerParams(
            collective_id=0, has_side_effects=True, vmem_limit_bytes=42 * 1024 * 1024
        ),
        name="adjoint_steps",
    )(
        signs,
        rec_owner.reshape(1, recv_dev),
        rec_cell.reshape(1, recv_dev),
        table,
        *mats,
        p_prev, p_cur, courant, snapshots, residual,
    )
    return pl.pallas_call(
        last_kernel,
        out_shape=(whole, whole),
        in_specs=[vmem] * len(state) + [anywhere] * 2,
        out_specs=(anywhere, anywhere),
        scratch_shapes=[
            *mat_scratch[:2],
            pltpu.VMEM((CHUNK, nx, ny), F32),
            pltpu.VMEM((CHUNK, nx, ny), F32),
            dma((2,)),
            dma((2 * chunks + 2 * (CHUNK // GROUP),)),
        ],
        compiler_params=pltpu.CompilerParams(vmem_limit_bytes=8 * 1024 * 1024),
        name="last_chunk",
    )(*held, *mats[:2])


def solution(mesh):
    placed = (
        P(None, "gx", "gy"),
        P(None, "gx", "gy"),
        P(None, "gx", "gy"),
        P(None, None, "gx", "gy"),
        P(None, ("gx", "gy"), None),
        P(("gx", "gy"), None),
        P(("gx", "gy")),
        P(),
    )
    return jax.shard_map(
        functools.partial(shards, mesh.shape["gx"], mesh.shape["gy"]),
        mesh=mesh,
        in_specs=placed,
        out_specs=(P(None, "gx", "gy"), P(None, "gx", "gy")),
        check_vma=False,
    )
```

```python
import functools
import math

import jax
import jax.numpy as jnp
import numpy as np
from jax import lax
from jax.experimental import pallas as pl
from jax.experimental.pallas import tpu as pltpu
from jax.sharding import PartitionSpec as P

STEPS = 3
NT = 128
RECV_DEPTH = 2
HALO = 4
CHUNK = 16
BLOCK = 256
GROUP = 8
SENDERS = 8

SCALE = 5040.0
CENTER_Y, CENTER_X = -43008.0, -42.0
TAPS = (8064.0, -1008.0, 128.0, -9.0)

F32 = jnp.float32
BF16 = jnp.bfloat16
I32 = jnp.int32
MESH = pl.DeviceIdType.MESH


def taps(distance):
    out = jnp.zeros(distance.shape, F32)
    for i, c in enumerate(TAPS):
        out = jnp.where(distance == i + 1, c, out)
    return out


def pieces(v):
    hi = v.astype(BF16)
    return hi, (v - hi.astype(F32)).astype(BF16)


def iota(shape, dim):
    return lax.broadcasted_iota(I32, shape, dim)


def lanes_dot(a, b, **kw):
    return lax.dot_general(a, b, (((1,), (1,)), ((), ())), preferred_element_type=F32, **kw)


def side_taps(nx):
    row = iota((16, 16), 0)
    src = iota((16, 16), 1) & 7
    place = jnp.where(src < 4, src - 4, nx + src - 4)
    target = jnp.where(row < 8, row, nx - 16 + row)
    return taps(jnp.abs(place - target)).astype(BF16)


def border_of(h_x, overs):
    cols = []
    for over in overs:
        hi, lo = pieces(over)
        cols.append(jnp.concatenate([hi.astype(F32), lo.astype(F32)], axis=0).astype(BF16))
    return jnp.dot(h_x, jnp.concatenate(cols, axis=1), preferred_element_type=F32)


def lateral(t_x, t_y, vs):
    (hi0, lo0), (hi1, lo1) = pieces(vs[0]), pieces(vs[1])
    hi = jnp.concatenate([hi0, hi1], axis=1)
    lo = jnp.concatenate([lo0, lo1], axis=1)
    return jnp.dot(
        jnp.concatenate([hi, lo, t_x[...]], axis=1),
        jnp.concatenate([t_y[...], t_y[...], hi, lo], axis=0),
        preferred_element_type=F32,
    )


def deep(cur, at):
    depth = TAPS[0] * (cur[at + 1] + cur[at - 1])
    for r in range(2, HALO + 1):
        depth = depth + TAPS[r - 1] * (cur[at + r] + cur[at - r])
    return depth


def with_border(lap, border):
    nx = lap.shape[0]
    return jnp.concatenate([lap[:8] + border[:8], lap[8 : nx - 8], lap[nx - 8 :] + border[8:]], axis=0)


def gather_edges(vs):
    lane = iota(vs[0].shape, 1)
    width = 1
    while len(vs) > 1:
        inside = (lane >= 8 * width - 4) & (lane < 16 * width - 4)
        vs = [
            jnp.where(inside, pltpu.roll(b, 8 * width, 1), a) for a, b in zip(vs[::2], vs[1::2])
        ]
        width *= 2
    return vs[0]


def to_sides(first, second):
    nx, ny = first.shape
    half = nx // 2
    lane = iota((nx, ny), 1)
    whole = jnp.where((lane >= ny // 2 - 4) & (lane < ny - 4), pltpu.roll(second, ny // 2, 1), first)
    top, low = whole[:half], pltpu.roll(whole[half:], 4, 1)
    odd = (iota((half, ny), 1) & 4) != 0
    return jnp.where(odd, top, low), jnp.where(odd, low, top)


def edge_terms(left, right, onto):
    half, ny = left.shape
    odd = (iota((half, ny), 1) & 4) != 0
    edges = jnp.concatenate(
        [jnp.where(odd, left, right), pltpu.roll(jnp.where(odd, right, left), ny - 4, 1)], axis=0
    )
    return jnp.dot(
        jnp.concatenate(pieces(edges), axis=1), jnp.concatenate([onto[...]] * 2, axis=0),
        preferred_element_type=F32,
    )


def placed_edge(terms, q):
    nx, ny = terms.shape
    lane = iota((nx, ny), 1)
    turned = pltpu.roll(terms, (2 * ny - 4 - 8 * q) & (ny - 1), 1)
    return jnp.where((lane < HALO) | (lane >= ny - HALO), turned, 0.0)


def main_kernel(
    n_gx, n_gy, signs, owner_h, cell_h, table_h, t_x_h, t_y_h, onto_h,
    p_prev, p_cur, courant_h, snaps_h, residual_h,
    buf_a, buf_b, courant, snaps, image, edge_out, over_out, source_out,
    owner, cell, table, t_x, t_y, onto, residual, sx, rx, sy, ry, edge, planes, packed,
    snd, got, load_sem, sxs, rxs, sys_, rys, snds, gots,
):
    n = n_gx * n_gy
    nz, nx, ny = p_cur.shape
    half, mid = nx // 2, ny // 2
    chunks = nz // CHUNK
    deeper = tuple(range(chunks - 1, 0, -1))
    gx, gy = lax.axis_index("gx"), lax.axis_index("gy")
    me = gx * n_gy + gy

    inner = pl.ds(HALO, nz)
    plan = [
        (p_cur, buf_a.at[inner]), (residual_h, residual), (owner_h, owner), (cell_h, cell), (table_h, table),
        (t_x_h, t_x), (t_y_h, t_y), (p_prev, buf_b.at[inner]), (courant_h, courant), (onto_h, onto),
        (snaps_h, snaps),
    ]
    loads = [pltpu.make_async_copy(s, d, load_sem.at[i]) for i, (s, d) in enumerate(plan)]
    for load in loads:
        load.start()

    barrier = pltpu.get_barrier_semaphore()

    def greet(o, carry):
        d = lax.rem(me + o, n)
        pl.semaphore_signal(
            barrier, inc=1, device_id=(d // n_gy, lax.rem(d, n_gy)), device_id_type=MESH
        )
        return carry

    lax.fori_loop(1, n, greet, 0)

    h_x = side_taps(nx)
    zero = jnp.zeros((HALO, nx, ny), F32)
    for buf in (buf_a, buf_b):
        buf[pl.ds(0, HALO)] = zero
        buf[pl.ds(HALO + nz, HALO)] = zero

    for side, absent in ((0, gx == 0), (1, gx == n_gx - 1)):

        @pl.when(absent)
        def _(side=side):
            for k in range(STEPS):
                rx[k, side] = jnp.zeros(rx.shape[2:], F32)

    for side, absent in ((0, gy == 0), (1, gy == n_gy - 1)):

        @pl.when(absent)
        def _(side=side):
            for k in range(STEPS):
                ry[k, side] = jnp.zeros(ry.shape[2:], F32)

    def pack(vs, k, g, j):
        for i, v in enumerate(vs):
            z = g * CHUNK + GROUP * j + i
            sx[k, 0, z] = v[nx - HALO :]
            sx[k, 1, z] = v[:HALO]
        packed[k % 2, j] = gather_edges(vs)

    def settle(k, g):
        sy[k, 0, g], sy[k, 1, g] = to_sides(packed[k % 2, 0], packed[k % 2, 1])

    def halo_copies(k, g):
        zs = pl.ds(g * CHUNK, CHUNK)
        out = []
        for side, step, send_ok, recv_ok in (
            (0, 1, gy < n_gy - 1, gy > 0),
            (1, -1, gy > 0, gy < n_gy - 1),
        ):
            i = (k * chunks + g) * 2 + side
            copy = pltpu.make_async_remote_copy(
                src_ref=sy.at[k, side, g], dst_ref=ry.at[k, side, g],
                send_sem=sys_.at[i], recv_sem=rys.at[i],
                device_id=(gx, lax.rem(gy + step + n_gy, n_gy)), device_id_type=MESH,
            )
            out.append((copy, send_ok, recv_ok))
        for side, step, send_ok, recv_ok in (
            (0, 1, gx < n_gx - 1, gx > 0),
            (1, -1, gx > 0, gx < n_gx - 1),
        ):
            i = (k * chunks + g) * 2 + side
            copy = pltpu.make_async_remote_copy(
                src_ref=sx.at[k, side, zs], dst_ref=rx.at[k, side, zs],
                send_sem=sxs.at[i], recv_sem=rxs.at[i],
                device_id=(lax.rem(gx + step + n_gx, n_gx), gy), device_id_type=MESH,
            )
            out.append((copy, send_ok, recv_ok))
        return out

    def send_halo(k, g):
        for copy, send_ok, _ in halo_copies(k, g):
            pl.when(send_ok)(copy.start)

    def wait_halo(k, g):
        for copy, _, recv_ok in halo_copies(k, g):
            pl.when(recv_ok)(copy.wait_recv)

    def each(body):
        lax.fori_loop(0, CHUNK // GROUP, lambda j, c: (body(j), c)[1], 0)

    def beyond(k, z):
        return jnp.concatenate([rx[k, 0, z], rx[k, 1, z]], axis=0)

    loads[0].wait()
    for g in range(chunks):

        def first_pack(j, g=g):
            pack([buf_a[HALO + g * CHUNK + GROUP * j + i] for i in range(GROUP)], 0, g, j)

        each(first_pack)
        settle(0, g)

    pl.semaphore_wait(barrier, n - 1)
    for g in deeper + (0,):
        send_halo(0, g)

    for load in loads[1:5]:
        load.wait()
    recv_dev = owner.shape[1]
    slots = snd.shape[2]
    upper = (iota((BLOCK, BLOCK), 0) < iota((BLOCK, BLOCK), 1)).astype(F32).astype(BF16)
    count = jnp.zeros((n, 1), F32)
    message = jnp.zeros((n * 8, slots), F32)
    part = iota((8, BLOCK), 0)
    shift = ny.bit_length() - 1
    for blk in range(recv_dev // BLOCK):
        rows = pl.ds(blk * BLOCK, BLOCK)
        enc = signs[0].astype(F32) * residual[0, rows, :]
        for s in range(1, residual.shape[0]):
            enc = enc + signs[s].astype(F32) * residual[s, rows, :]
        both = lanes_dot(table[...], jnp.concatenate(pieces(enc), axis=1))
        amps = both[:8] + both[8:]
        hi = amps.astype(BF16).astype(F32)
        c = cell[:, rows]
        at_x = (c >> shift).astype(F32)
        at_y = (c & (ny - 1)).astype(F32)
        payload = jnp.where((part & 1) == 0, hi, amps - hi)
        payload = jnp.where(part == 6, at_x, payload)
        payload = jnp.where(part == 7, at_y, payload)
        onehot = jnp.where(iota((n, BLOCK), 0) == owner[:, rows], 1.0, 0.0)
        before = jnp.dot(onehot.astype(BF16), upper, preferred_element_type=F32) + count
        count = count + jnp.sum(onehot, axis=1, keepdims=True)
        rank = jnp.sum(before * onehot, axis=0, keepdims=True)
        spread = (onehot[:, None, :] * payload[None]).reshape(n * 8, BLOCK).astype(BF16)
        slot = jnp.where(iota((slots, BLOCK), 0).astype(F32) == rank, 1.0, 0.0).astype(BF16)
        message = message + lanes_dot(spread, slot)
    snd[...] = message.reshape(n, 8, slots)
    got[me] = snd[me]

    def message_to(o):
        d = lax.rem(me + o, n)
        return pltpu.make_async_remote_copy(
            src_ref=snd.at[d], dst_ref=got.at[me], send_sem=snds.at[o], recv_sem=gots.at[o],
            device_id=(d // n_gy, lax.rem(d, n_gy)), device_id_type=MESH,
        )

    def post(o, carry):
        message_to(o).start()
        return carry

    def step_chunk(k, g, inside=False):
        cur, prev = (buf_a, buf_b) if k % 2 == 0 else (buf_b, buf_a)
        if not inside:
            wait_halo(k, g)
            edge[...] = edge_terms(ry[k, 0, g], ry[k, 1, g], onto)

        def body(j):
            qs = [GROUP * j + i for i in range(GROUP)]
            made = []
            for p in range(GROUP // 2):
                pair = qs[2 * p : 2 * p + 2]
                zs = [g * CHUNK + q for q in pair]
                vs = [cur[z + HALO] for z in zs]
                lap2 = lateral(t_x, t_y, vs)
                border2 = None if inside else border_of(h_x, [beyond(k, z) for z in zs])
                for i, (z, v) in enumerate(zip(zs, vs)):
                    cols = slice(i * ny, (i + 1) * ny)
                    lap = lap2[:, cols] + deep(cur, z + HALO)
                    if not inside:
                        lap = with_border(lap + placed_edge(edge[...], pair[i]), border2[:, cols])
                    if k == 0:
                        speed = courant[z] * (1.0 / SCALE)
                        courant[z] = speed
                    else:
                        speed = courant[z]
                    old = prev[z + HALO]
                    nxt = (2.0 * v - old) + speed * lap
                    if k == STEPS - 1:
                        image[z] = (
                            snaps[0, z].astype(F32) * old + snaps[1, z].astype(F32) * v
                            + snaps[2, z].astype(F32) * nxt
                        )
                    prev[z + HALO] = nxt
                    made.append(nxt)
            if k < STEPS - 1 and not inside:
                pack(made, k + 1, g, j)

        each(body)
        if k < STEPS - 1 and not inside and (k, g) != (0, 0):
            settle(k + 1, g)

    def complete(g):
        wait_halo(0, g)
        edge[...] = edge_terms(ry[0, 0, g], ry[0, 1, g], onto)

        def body(j):
            qs = [GROUP * j + i for i in range(GROUP)]
            made = []
            for p in range(GROUP // 2):
                zs = [g * CHUNK + q for q in qs[2 * p : 2 * p + 2]]
                border2 = border_of(h_x, [beyond(0, z) for z in zs])
                for i, z in enumerate(zs):
                    cols = slice(i * ny, (i + 1) * ny)
                    lap = with_border(placed_edge(edge[...], qs[2 * p + i]), border2[:, cols])
                    nxt = buf_b[z + HALO] + courant[z] * lap
                    buf_b[z + HALO] = nxt
                    made.append(nxt)
            pack(made, 1, g, j)

        each(body)
        settle(1, g)
        send_halo(1, g)

    lax.fori_loop(1, n, post, 0)
    for load in loads[5:9]:
        load.wait()
    for g in deeper:
        step_chunk(0, g, inside=True)
    loads[9].wait()
    for g in deeper:
        complete(g)
    step_chunk(0, 0)

    def arrive(o, carry):
        d = lax.rem(me - o + n, n)
        pltpu.make_async_remote_copy(
            src_ref=snd.at[d], dst_ref=got.at[d], send_sem=snds.at[o], recv_sem=gots.at[o],
            device_id=(d // n_gy, lax.rem(d, n_gy)), device_id_type=MESH,
        ).wait_recv()
        return carry

    lax.fori_loop(1, n, arrive, 0)
    planes[...] = jnp.zeros(planes.shape, F32)
    row_x = iota((nx, slots), 0).astype(F32)
    row_y = iota((ny, slots), 0).astype(F32)

    def gather(j, carry):
        lhs, rhs = [], [[] for _ in range(2 * STEPS)]
        for i in range(SENDERS):
            block = got[SENDERS * j + i]
            lhs.append(jnp.where(row_x == block[6:7], 1.0, 0.0).astype(BF16))
            at_y = row_y == block[7:8]
            for h in range(2 * STEPS):
                rhs[h].append(jnp.where(at_y, block[h : h + 1], 0.0).astype(BF16))
        rhs = jnp.concatenate([jnp.concatenate(r, axis=1) for r in rhs], axis=0)
        planes[...] += lanes_dot(jnp.concatenate(lhs, axis=1), rhs)
        return carry

    lax.fori_loop(0, n // SENDERS, gather, 0)

    def source(k):
        cols = planes[:, 2 * k * ny : (2 * k + 2) * ny]
        return (SCALE * courant[RECV_DEPTH]) * (cols[:, :ny] + cols[:, ny:])

    at = HALO + RECV_DEPTH
    fixed = buf_b[at] + source(0)
    buf_b[at] = fixed
    sx[1, 0, RECV_DEPTH] = fixed[nx - HALO :]
    sx[1, 1, RECV_DEPTH] = fixed[:HALO]
    near = 8 * RECV_DEPTH - 4
    lane = iota((nx, ny), 1)
    packed[1, 0] = jnp.where(
        (lane >= near) & (lane < near + 8), pltpu.roll(fixed, 8 * RECV_DEPTH, 1), packed[1, 0]
    )
    settle(1, 0)
    send_halo(1, 0)
    for g in deeper:
        step_chunk(1, g)
        send_halo(2, g)
    buf_a[at] = buf_a[at] - source(1)
    step_chunk(1, 0)
    send_halo(2, 0)
    loads[10].wait()
    for g in deeper:
        step_chunk(2, g)
    source_out[...] = source(2)
    wait_halo(2, 0)
    edge_out[...] = edge_terms(ry[2, 0, 0], ry[2, 1, 0], onto)
    over_out[:, :HALO] = rx[2, 0, pl.ds(0, CHUNK)]
    over_out[:, HALO:] = rx[2, 1, pl.ds(0, CHUNK)]

    def finish(o, carry):
        message_to(o).wait_send()
        return carry

    lax.fori_loop(1, n, finish, 0)
    for k in range(STEPS):
        for g in range(chunks):
            for copy, send_ok, _ in halo_copies(k, g):
                pl.when(send_ok)(copy.wait_send)


def last_kernel(
    buf_a, buf_b, courant, snaps, image, edge, over, source, t_x_h, t_y_h,
    field_out, image_out,
    t_x, t_y, field0, image0, load_sem, out_sem,
):
    nz, nx, ny = courant.shape
    chunks = nz // CHUNK
    loads = [
        pltpu.make_async_copy(s, d, load_sem.at[i])
        for i, (s, d) in enumerate(((t_x_h, t_x), (t_y_h, t_y)))
    ]
    for load in loads:
        load.start()
    outs = []
    for g in range(chunks - 1, 0, -1):
        zs = pl.ds(g * CHUNK, CHUNK)
        outs += [
            pltpu.make_async_copy(
                buf_b.at[pl.ds(HALO + g * CHUNK, CHUNK)], field_out.at[zs], out_sem.at[2 * g]
            ),
            pltpu.make_async_copy(image.at[zs], image_out.at[zs], out_sem.at[2 * g + 1]),
        ]
    for out in outs:
        out.start()
    h_x = side_taps(nx)
    for load in loads:
        load.wait()

    def rest(j):
        zs = pl.ds(j * GROUP, GROUP)
        return [
            pltpu.make_async_copy(field0.at[zs], field_out.at[zs], out_sem.at[2 * chunks + 2 * j]),
            pltpu.make_async_copy(image0.at[zs], image_out.at[zs], out_sem.at[2 * chunks + 2 * j + 1]),
        ]

    def body(j, carry):
        for p in range(GROUP // 2):
            zs = [GROUP * j + 2 * p + i for i in range(2)]
            vs = [buf_a[z + HALO] for z in zs]
            lap2 = lateral(t_x, t_y, vs)
            border2 = border_of(h_x, [over[z] for z in zs])
            for i, (z, v) in enumerate(zip(zs, vs)):
                cols = slice(i * ny, (i + 1) * ny)
                lap = lap2[:, cols] + deep(buf_a, z + HALO) + placed_edge(edge[...], z)
                lap = with_border(lap, border2[:, cols])
                old = buf_b[z + HALO]
                nxt = (2.0 * v - old) + courant[z] * lap
                nxt = nxt + jnp.where(z == RECV_DEPTH, source[...], 0.0)
                field0[z] = nxt
                image0[z] = (
                    snaps[0, z].astype(F32) * old + snaps[1, z].astype(F32) * v
                    + snaps[2, z].astype(F32) * nxt
                )
        for out in rest(j):
            out.start()
        return carry

    lax.fori_loop(0, CHUNK // GROUP, body, 0)
    for j in range(CHUNK // GROUP):
        for out in rest(j):
            out.wait()
    for out in outs:
        out.wait()


def step_table(samples, steps):
    rows = np.arange(samples, dtype=np.float64)[None, :]
    cols = np.repeat(np.arange(steps, dtype=np.float64), 2)[:, None]
    table = np.cos(math.pi * (cols + 0.5) * (rows + 0.5) / samples) * math.sqrt(2.0 / samples)
    table = np.concatenate([table, np.zeros((8 - 2 * steps, samples))]).astype(np.float32)
    hi = table.astype(jnp.bfloat16)
    lo = (table - hi.astype(np.float32)).astype(jnp.bfloat16)
    return np.concatenate(
        [np.concatenate([hi, hi], axis=1), np.concatenate([lo, np.zeros_like(lo)], axis=1)], axis=0
    )


def tap_values(distance):
    out = np.zeros(distance.shape, np.float32)
    for i, c in enumerate(TAPS):
        out[distance == i + 1] = c
    return out


def band(size, center):
    a = np.arange(size)
    distance = np.abs(a[:, None] - a[None, :])
    return np.where(distance == 0, np.float32(center), tap_values(distance))


def matrices(nx, ny):
    t_x = np.concatenate([band(nx, CENTER_X)] * 2, axis=1)
    t_y = np.zeros((2 * ny, 2 * ny), np.float32)
    t_y[:ny, :ny] = t_y[ny:, ny:] = band(ny, CENTER_Y)
    a, b = np.arange(ny)[:, None], np.arange(ny)[None, :]
    left = (a & 4) != 0
    place = np.where(left, (a & 3) - 4, ny + (a & 3))
    plane = np.where(left, (a + 4) % ny, a) >> 3
    target = np.where((b & 7) < 4, ny - 4 + (b & 7), (b & 7) - 4)
    onto = np.where(plane == b >> 3, tap_values(np.abs(place - target)), np.float32(0))
    return [jnp.asarray(m.astype(jnp.bfloat16)) for m in (t_x, t_y, onto)]


def shards(n_gx, n_gy, p_prev, p_cur, courant, snapshots, residual, rec_owner, rec_cell, signs):
    nz, nx, ny = p_cur.shape
    n = n_gx * n_gy
    recv_dev = rec_cell.shape[0]
    slots = -(-(2 * recv_dev // n) // 128) * 128
    chunks = nz // CHUNK
    anywhere = pl.BlockSpec(memory_space=pl.ANY)
    vmem = pl.BlockSpec(memory_space=pltpu.VMEM)
    dma = pltpu.SemaphoreType.DMA
    whole = jax.ShapeDtypeStruct(p_cur.shape, F32)
    mats = matrices(nx, ny)
    mat_scratch = [pltpu.VMEM(m.shape, BF16) for m in mats]
    table = jnp.asarray(step_table(NT, STEPS))
    state = (
        pltpu.VMEM((nz + 2 * HALO, nx, ny), F32),
        pltpu.VMEM((nz + 2 * HALO, nx, ny), F32),
        pltpu.VMEM((nz, nx, ny), F32),
        pltpu.VMEM((STEPS, nz, nx, ny), BF16),
        pltpu.VMEM((nz, nx, ny), F32),
        pltpu.VMEM((nx, ny), F32),
        pltpu.VMEM((CHUNK, 2 * HALO, ny), F32),
        pltpu.VMEM((nx, ny), F32),
    )
    held = pl.pallas_call(
        functools.partial(main_kernel, n_gx, n_gy),
        out_shape=state,
        in_specs=[pl.BlockSpec(memory_space=pltpu.SMEM)] + [anywhere] * 11,
        out_specs=(vmem,) * len(state),
        scratch_shapes=[
            pltpu.VMEM((1, recv_dev), I32),
            pltpu.VMEM((1, recv_dev), I32),
            pltpu.VMEM(table.shape, BF16),
            *mat_scratch,
            pltpu.VMEM(residual.shape, F32),
            pltpu.VMEM((STEPS, 2, nz, HALO, ny), F32),
            pltpu.VMEM((STEPS, 2, nz, HALO, ny), F32),
            pltpu.VMEM((STEPS, 2, chunks, nx // 2, ny), F32),
            pltpu.VMEM((STEPS, 2, chunks, nx // 2, ny), F32),
            pltpu.VMEM((nx, ny), F32),
            pltpu.VMEM((nx, 2 * STEPS * ny), F32),
            pltpu.VMEM((2, CHUNK // GROUP, nx, ny), F32),
            pltpu.VMEM((n, 8, slots), F32),
            pltpu.VMEM((n, 8, slots), F32),
            dma((11,)),
            dma((2 * STEPS * chunks,)),
            dma((2 * STEPS * chunks,)),
            dma((2 * STEPS * chunks,)),
            dma((2 * STEPS * chunks,)),
            dma((n,)),
            dma((n,)),
        ],
        compiler_params=pltpu.CompilerParams(
            collective_id=0, has_side_effects=True, vmem_limit_bytes=42 * 1024 * 1024
        ),
        name="adjoint_steps",
    )(
        signs,
        rec_owner.reshape(1, recv_dev),
        rec_cell.reshape(1, recv_dev),
        table,
        *mats,
        p_prev, p_cur, courant, snapshots, residual,
    )
    return pl.pallas_call(
        last_kernel,
        out_shape=(whole, whole),
        in_specs=[vmem] * len(state) + [anywhere] * 2,
        out_specs=(anywhere, anywhere),
        scratch_shapes=[
            *mat_scratch[:2],
            pltpu.VMEM((CHUNK, nx, ny), F32),
            pltpu.VMEM((CHUNK, nx, ny), F32),
            dma((2,)),
            dma((2 * chunks + 2 * (CHUNK // GROUP),)),
        ],
        compiler_params=pltpu.CompilerParams(vmem_limit_bytes=8 * 1024 * 1024),
        name="last_chunk",
    )(*held, *mats[:2])


def solution(mesh):
    placed = (
        P(None, "gx", "gy"),
        P(None, "gx", "gy"),
        P(None, "gx", "gy"),
        P(None, None, "gx", "gy"),
        P(None, ("gx", "gy"), None),
        P(("gx", "gy"), None),
        P(("gx", "gy")),
        P(),
    )
    return jax.shard_map(
        functools.partial(shards, mesh.shape["gx"], mesh.shape["gy"]),
        mesh=mesh,
        in_specs=placed,
        out_specs=(P(None, "gx", "gy"), P(None, "gx", "gy")),
        check_vma=False,
    )
```

```python
import functools
import math

import jax
import jax.numpy as jnp
import numpy as np
from jax import lax
from jax.experimental import pallas as pl
from jax.experimental.pallas import tpu as pltpu
from jax.sharding import PartitionSpec as P

STEPS = 3
NT = 128
RECV_DEPTH = 2
HALO = 4
CHUNK = 16
BLOCK = 256
GROUP = 8
SENDERS = 8

SCALE = 5040.0
CENTER_Y, CENTER_X = -43008.0, -42.0
TAPS = (8064.0, -1008.0, 128.0, -9.0)

F32 = jnp.float32
BF16 = jnp.bfloat16
I32 = jnp.int32
MESH = pl.DeviceIdType.MESH


def taps(distance):
    out = jnp.zeros(distance.shape, F32)
    for i, c in enumerate(TAPS):
        out = jnp.where(distance == i + 1, c, out)
    return out


def pieces(v):
    hi = v.astype(BF16)
    return hi, (v - hi.astype(F32)).astype(BF16)


def iota(shape, dim):
    return lax.broadcasted_iota(I32, shape, dim)


def lanes_dot(a, b, **kw):
    return lax.dot_general(a, b, (((1,), (1,)), ((), ())), preferred_element_type=F32, **kw)


def side_taps(nx):
    row = iota((16, 16), 0)
    src = iota((16, 16), 1) & 7
    place = jnp.where(src < 4, src - 4, nx + src - 4)
    target = jnp.where(row < 8, row, nx - 16 + row)
    return taps(jnp.abs(place - target)).astype(BF16)


def border_of(h_x, overs):
    cols = []
    for over in overs:
        hi, lo = pieces(over)
        cols.append(jnp.concatenate([hi.astype(F32), lo.astype(F32)], axis=0).astype(BF16))
    return jnp.dot(h_x, jnp.concatenate(cols, axis=1), preferred_element_type=F32)


def lateral(t_x, t_y, vs):
    (hi0, lo0), (hi1, lo1) = pieces(vs[0]), pieces(vs[1])
    hi = jnp.concatenate([hi0, hi1], axis=1)
    lo = jnp.concatenate([lo0, lo1], axis=1)
    return jnp.dot(
        jnp.concatenate([hi, lo, t_x[...]], axis=1),
        jnp.concatenate([t_y[...], t_y[...], hi, lo], axis=0),
        preferred_element_type=F32,
    )


def deep(cur, at):
    depth = TAPS[0] * (cur[at + 1] + cur[at - 1])
    for r in range(2, HALO + 1):
        depth = depth + TAPS[r - 1] * (cur[at + r] + cur[at - r])
    return depth


def with_border(lap, border):
    nx = lap.shape[0]
    return jnp.concatenate([lap[:8] + border[:8], lap[8 : nx - 8], lap[nx - 8 :] + border[8:]], axis=0)


def gather_edges(vs):
    lane = iota(vs[0].shape, 1)
    width = 1
    while len(vs) > 1:
        inside = (lane >= 8 * width - 4) & (lane < 16 * width - 4)
        vs = [
            jnp.where(inside, pltpu.roll(b, 8 * width, 1), a) for a, b in zip(vs[::2], vs[1::2])
        ]
        width *= 2
    return vs[0]


def to_sides(first, second):
    nx, ny = first.shape
    half = nx // 2
    lane = iota((nx, ny), 1)
    whole = jnp.where((lane >= ny // 2 - 4) & (lane < ny - 4), pltpu.roll(second, ny // 2, 1), first)
    top, low = whole[:half], pltpu.roll(whole[half:], 4, 1)
    odd = (iota((half, ny), 1) & 4) != 0
    return jnp.where(odd, top, low), jnp.where(odd, low, top)


def edge_terms(left, right, onto):
    half, ny = left.shape
    odd = (iota((half, ny), 1) & 4) != 0
    edges = jnp.concatenate(
        [jnp.where(odd, left, right), pltpu.roll(jnp.where(odd, right, left), ny - 4, 1)], axis=0
    )
    return jnp.dot(
        jnp.concatenate(pieces(edges), axis=1), jnp.concatenate([onto[...]] * 2, axis=0),
        preferred_element_type=F32,
    )


def placed_edge(terms, q):
    nx, ny = terms.shape
    lane = iota((nx, ny), 1)
    turned = pltpu.roll(terms, (2 * ny - 4 - 8 * q) & (ny - 1), 1)
    return jnp.where((lane < HALO) | (lane >= ny - HALO), turned, 0.0)


def main_kernel(
    n_gx, n_gy, signs, owner_h, cell_h, table_h, t_x_h, t_y_h, onto_h,
    p_prev, p_cur, courant_h, snaps_h, residual_h,
    buf_a, buf_b, courant, snaps, image, edge_out, over_out, source_out,
    owner, cell, table, t_x, t_y, onto, residual, sx, rx, sy, ry, edge, planes, packed,
    snd, got, load_sem, sxs, rxs, sys_, rys, snds, gots,
):
    n = n_gx * n_gy
    nz, nx, ny = p_cur.shape
    half, mid = nx // 2, ny // 2
    chunks = nz // CHUNK
    deeper = tuple(range(chunks - 1, 0, -1))
    gx, gy = lax.axis_index("gx"), lax.axis_index("gy")
    me = gx * n_gy + gy

    inner = pl.ds(HALO, nz)
    plan = [
        (p_cur, buf_a.at[inner]), (residual_h, residual), (owner_h, owner), (cell_h, cell), (table_h, table),
        (t_x_h, t_x), (t_y_h, t_y), (p_prev, buf_b.at[inner]), (courant_h, courant), (onto_h, onto),
        (snaps_h, snaps),
    ]
    loads = [pltpu.make_async_copy(s, d, load_sem.at[i]) for i, (s, d) in enumerate(plan)]
    for load in loads:
        load.start()

    barrier = pltpu.get_barrier_semaphore()

    def greet(o, carry):
        d = lax.rem(me + o, n)
        pl.semaphore_signal(
            barrier, inc=1, device_id=(d // n_gy, lax.rem(d, n_gy)), device_id_type=MESH
        )
        return carry

    lax.fori_loop(1, n, greet, 0)

    h_x = side_taps(nx)
    zero = jnp.zeros((HALO, nx, ny), F32)
    for buf in (buf_a, buf_b):
        buf[pl.ds(0, HALO)] = zero
        buf[pl.ds(HALO + nz, HALO)] = zero

    for side, absent in ((0, gx == 0), (1, gx == n_gx - 1)):

        @pl.when(absent)
        def _(side=side):
            for k in range(STEPS):
                rx[k, side] = jnp.zeros(rx.shape[2:], F32)

    for side, absent in ((0, gy == 0), (1, gy == n_gy - 1)):

        @pl.when(absent)
        def _(side=side):
            for k in range(STEPS):
                ry[k, side] = jnp.zeros(ry.shape[2:], F32)

    def pack(vs, k, g, j):
        for i, v in enumerate(vs):
            z = g * CHUNK + GROUP * j + i
            sx[k, 0, z] = v[nx - HALO :]
            sx[k, 1, z] = v[:HALO]
        packed[k % 2, j] = gather_edges(vs)

    def settle(k, g):
        sy[k, 0, g], sy[k, 1, g] = to_sides(packed[k % 2, 0], packed[k % 2, 1])

    def halo_copies(k, g):
        zs = pl.ds(g * CHUNK, CHUNK)
        out = []
        for side, step, send_ok, recv_ok in (
            (0, 1, gy < n_gy - 1, gy > 0),
            (1, -1, gy > 0, gy < n_gy - 1),
        ):
            i = (k * chunks + g) * 2 + side
            copy = pltpu.make_async_remote_copy(
                src_ref=sy.at[k, side, g], dst_ref=ry.at[k, side, g],
                send_sem=sys_.at[i], recv_sem=rys.at[i],
                device_id=(gx, lax.rem(gy + step + n_gy, n_gy)), device_id_type=MESH,
            )
            out.append((copy, send_ok, recv_ok))
        for side, step, send_ok, recv_ok in (
            (0, 1, gx < n_gx - 1, gx > 0),
            (1, -1, gx > 0, gx < n_gx - 1),
        ):
            i = (k * chunks + g) * 2 + side
            copy = pltpu.make_async_remote_copy(
                src_ref=sx.at[k, side, zs], dst_ref=rx.at[k, side, zs],
                send_sem=sxs.at[i], recv_sem=rxs.at[i],
                device_id=(lax.rem(gx + step + n_gx, n_gx), gy), device_id_type=MESH,
            )
            out.append((copy, send_ok, recv_ok))
        return out

    def send_halo(k, g):
        for copy, send_ok, _ in halo_copies(k, g):
            pl.when(send_ok)(copy.start)

    def wait_halo(k, g):
        for copy, _, recv_ok in halo_copies(k, g):
            pl.when(recv_ok)(copy.wait_recv)

    def each(body):
        lax.fori_loop(0, CHUNK // GROUP, lambda j, c: (body(j), c)[1], 0)

    def beyond(k, z):
        return jnp.concatenate([rx[k, 0, z], rx[k, 1, z]], axis=0)

    loads[0].wait()
    for g in range(chunks):

        def first_pack(j, g=g):
            pack([buf_a[HALO + g * CHUNK + GROUP * j + i] for i in range(GROUP)], 0, g, j)

        each(first_pack)
        settle(0, g)

    pl.semaphore_wait(barrier, n - 1)
    for g in deeper + (0,):
        send_halo(0, g)

    for load in loads[1:5]:
        load.wait()
    recv_dev = owner.shape[1]
    slots = snd.shape[2]
    upper = (iota((BLOCK, BLOCK), 0) < iota((BLOCK, BLOCK), 1)).astype(F32).astype(BF16)
    count = jnp.zeros((n, 1), F32)
    message = jnp.zeros((n * 8, slots), F32)
    part = iota((8, BLOCK), 0)
    shift = ny.bit_length() - 1
    for blk in range(recv_dev // BLOCK):
        rows = pl.ds(blk * BLOCK, BLOCK)
        enc = signs[0].astype(F32) * residual[0, rows, :]
        for s in range(1, residual.shape[0]):
            enc = enc + signs[s].astype(F32) * residual[s, rows, :]
        both = lanes_dot(table[...], jnp.concatenate(pieces(enc), axis=1))
        amps = both[:8] + both[8:]
        hi = amps.astype(BF16).astype(F32)
        c = cell[:, rows]
        at_x = (c >> shift).astype(F32)
        at_y = (c & (ny - 1)).astype(F32)
        payload = jnp.where((part & 1) == 0, hi, amps - hi)
        payload = jnp.where(part == 6, at_x, payload)
        payload = jnp.where(part == 7, at_y, payload)
        onehot = jnp.where(iota((n, BLOCK), 0) == owner[:, rows], 1.0, 0.0)
        before = jnp.dot(onehot.astype(BF16), upper, preferred_element_type=F32) + count
        count = count + jnp.sum(onehot, axis=1, keepdims=True)
        rank = jnp.sum(before * onehot, axis=0, keepdims=True)
        spread = (onehot[:, None, :] * payload[None]).reshape(n * 8, BLOCK).astype(BF16)
        slot = jnp.where(iota((slots, BLOCK), 0).astype(F32) == rank, 1.0, 0.0).astype(BF16)
        message = message + lanes_dot(spread, slot)
    snd[...] = message.reshape(n, 8, slots)
    got[me] = snd[me]

    def message_to(o):
        d = lax.rem(me + o, n)
        return pltpu.make_async_remote_copy(
            src_ref=snd.at[d], dst_ref=got.at[me], send_sem=snds.at[o], recv_sem=gots.at[o],
            device_id=(d // n_gy, lax.rem(d, n_gy)), device_id_type=MESH,
        )

    def post(o, carry):
        message_to(o).start()
        return carry

    def step_chunk(k, g, inside=False):
        cur, prev = (buf_a, buf_b) if k % 2 == 0 else (buf_b, buf_a)
        if not inside:
            wait_halo(k, g)
            edge[...] = edge_terms(ry[k, 0, g], ry[k, 1, g], onto)

        def body(j):
            qs = [GROUP * j + i for i in range(GROUP)]
            made = []
            for p in range(GROUP // 2):
                pair = qs[2 * p : 2 * p + 2]
                zs = [g * CHUNK + q for q in pair]
                vs = [cur[z + HALO] for z in zs]
                lap2 = lateral(t_x, t_y, vs)
                border2 = None if inside else border_of(h_x, [beyond(k, z) for z in zs])
                for i, (z, v) in enumerate(zip(zs, vs)):
                    cols = slice(i * ny, (i + 1) * ny)
                    lap = lap2[:, cols] + deep(cur, z + HALO)
                    if not inside:
                        lap = with_border(lap + placed_edge(edge[...], pair[i]), border2[:, cols])
                    if k == 0:
                        speed = courant[z] * (1.0 / SCALE)
                        courant[z] = speed
                    else:
                        speed = courant[z]
                    old = prev[z + HALO]
                    nxt = (2.0 * v - old) + speed * lap
                    if k == STEPS - 1:
                        image[z] = (
                            snaps[0, z].astype(F32) * old + snaps[1, z].astype(F32) * v
                            + snaps[2, z].astype(F32) * nxt
                        )
                    prev[z + HALO] = nxt
                    made.append(nxt)
            if k < STEPS - 1 and not inside:
                pack(made, k + 1, g, j)

        each(body)
        if k < STEPS - 1 and not inside and (k, g) != (0, 0):
            settle(k + 1, g)

    def complete(g):
        wait_halo(0, g)
        edge[...] = edge_terms(ry[0, 0, g], ry[0, 1, g], onto)

        def body(j):
            qs = [GROUP * j + i for i in range(GROUP)]
            made = []
            for p in range(GROUP // 2):
                zs = [g * CHUNK + q for q in qs[2 * p : 2 * p + 2]]
                border2 = border_of(h_x, [beyond(0, z) for z in zs])
                for i, z in enumerate(zs):
                    cols = slice(i * ny, (i + 1) * ny)
                    lap = with_border(placed_edge(edge[...], qs[2 * p + i]), border2[:, cols])
                    nxt = buf_b[z + HALO] + courant[z] * lap
                    buf_b[z + HALO] = nxt
                    made.append(nxt)
            pack(made, 1, g, j)

        each(body)
        if g:
            settle(1, g)
            send_halo(1, g)

    lax.fori_loop(1, n, post, 0)
    for load in loads[5:9]:
        load.wait()
    for g in deeper + (0,):
        step_chunk(0, g, inside=True)
    loads[9].wait()
    for g in deeper:
        complete(g)
    complete(0)

    def arrive(o, carry):
        d = lax.rem(me - o + n, n)
        pltpu.make_async_remote_copy(
            src_ref=snd.at[d], dst_ref=got.at[d], send_sem=snds.at[o], recv_sem=gots.at[o],
            device_id=(d // n_gy, lax.rem(d, n_gy)), device_id_type=MESH,
        ).wait_recv()
        return carry

    lax.fori_loop(1, n, arrive, 0)
    planes[...] = jnp.zeros(planes.shape, F32)
    row_x = iota((nx, slots), 0).astype(F32)
    row_y = iota((ny, slots), 0).astype(F32)

    def gather(j, carry):
        lhs, rhs = [], [[] for _ in range(2 * STEPS)]
        for i in range(SENDERS):
            block = got[SENDERS * j + i]
            lhs.append(jnp.where(row_x == block[6:7], 1.0, 0.0).astype(BF16))
            at_y = row_y == block[7:8]
            for h in range(2 * STEPS):
                rhs[h].append(jnp.where(at_y, block[h : h + 1], 0.0).astype(BF16))
        rhs = jnp.concatenate([jnp.concatenate(r, axis=1) for r in rhs], axis=0)
        planes[...] += lanes_dot(jnp.concatenate(lhs, axis=1), rhs)
        return carry

    lax.fori_loop(0, n // SENDERS, gather, 0)

    def source(k):
        cols = planes[:, 2 * k * ny : (2 * k + 2) * ny]
        return (SCALE * courant[RECV_DEPTH]) * (cols[:, :ny] + cols[:, ny:])

    at = HALO + RECV_DEPTH
    fixed = buf_b[at] + source(0)
    buf_b[at] = fixed
    sx[1, 0, RECV_DEPTH] = fixed[nx - HALO :]
    sx[1, 1, RECV_DEPTH] = fixed[:HALO]
    near = 8 * RECV_DEPTH - 4
    lane = iota((nx, ny), 1)
    packed[1, 0] = jnp.where(
        (lane >= near) & (lane < near + 8), pltpu.roll(fixed, 8 * RECV_DEPTH, 1), packed[1, 0]
    )
    settle(1, 0)
    send_halo(1, 0)
    for g in deeper:
        step_chunk(1, g)
        send_halo(2, g)
    buf_a[at] = buf_a[at] - source(1)
    step_chunk(1, 0)
    send_halo(2, 0)
    loads[10].wait()
    for g in deeper:
        step_chunk(2, g)
    source_out[...] = source(2)
    wait_halo(2, 0)
    edge_out[...] = edge_terms(ry[2, 0, 0], ry[2, 1, 0], onto)
    over_out[:, :HALO] = rx[2, 0, pl.ds(0, CHUNK)]
    over_out[:, HALO:] = rx[2, 1, pl.ds(0, CHUNK)]

    def finish(o, carry):
        message_to(o).wait_send()
        return carry

    lax.fori_loop(1, n, finish, 0)
    for k in range(STEPS):
        for g in range(chunks):
            for copy, send_ok, _ in halo_copies(k, g):
                pl.when(send_ok)(copy.wait_send)


def last_kernel(
    buf_a, buf_b, courant, snaps, image, edge, over, source, t_x_h, t_y_h,
    field_out, image_out,
    t_x, t_y, field0, image0, load_sem, out_sem,
):
    nz, nx, ny = courant.shape
    chunks = nz // CHUNK
    loads = [
        pltpu.make_async_copy(s, d, load_sem.at[i])
        for i, (s, d) in enumerate(((t_x_h, t_x), (t_y_h, t_y)))
    ]
    for load in loads:
        load.start()
    outs = []
    for g in range(chunks - 1, 0, -1):
        zs = pl.ds(g * CHUNK, CHUNK)
        outs += [
            pltpu.make_async_copy(
                buf_b.at[pl.ds(HALO + g * CHUNK, CHUNK)], field_out.at[zs], out_sem.at[2 * g]
            ),
            pltpu.make_async_copy(image.at[zs], image_out.at[zs], out_sem.at[2 * g + 1]),
        ]
    for out in outs:
        out.start()
    h_x = side_taps(nx)
    for load in loads:
        load.wait()

    def rest(j):
        zs = pl.ds(j * GROUP, GROUP)
        return [
            pltpu.make_async_copy(field0.at[zs], field_out.at[zs], out_sem.at[2 * chunks + 2 * j]),
            pltpu.make_async_copy(image0.at[zs], image_out.at[zs], out_sem.at[2 * chunks + 2 * j + 1]),
        ]

    def body(j, carry):
        for p in range(GROUP // 2):
            zs = [GROUP * j + 2 * p + i for i in range(2)]
            vs = [buf_a[z + HALO] for z in zs]
            lap2 = lateral(t_x, t_y, vs)
            border2 = border_of(h_x, [over[z] for z in zs])
            for i, (z, v) in enumerate(zip(zs, vs)):
                cols = slice(i * ny, (i + 1) * ny)
                lap = lap2[:, cols] + deep(buf_a, z + HALO) + placed_edge(edge[...], z)
                lap = with_border(lap, border2[:, cols])
                old = buf_b[z + HALO]
                nxt = (2.0 * v - old) + courant[z] * lap
                nxt = nxt + jnp.where(z == RECV_DEPTH, source[...], 0.0)
                field0[z] = nxt
                image0[z] = (
                    snaps[0, z].astype(F32) * old + snaps[1, z].astype(F32) * v
                    + snaps[2, z].astype(F32) * nxt
                )
        for out in rest(j):
            out.start()
        return carry

    lax.fori_loop(0, CHUNK // GROUP, body, 0)
    for j in range(CHUNK // GROUP):
        for out in rest(j):
            out.wait()
    for out in outs:
        out.wait()


def step_table(samples, steps):
    rows = np.arange(samples, dtype=np.float64)[None, :]
    cols = np.repeat(np.arange(steps, dtype=np.float64), 2)[:, None]
    table = np.cos(math.pi * (cols + 0.5) * (rows + 0.5) / samples) * math.sqrt(2.0 / samples)
    table = np.concatenate([table, np.zeros((8 - 2 * steps, samples))]).astype(np.float32)
    hi = table.astype(jnp.bfloat16)
    lo = (table - hi.astype(np.float32)).astype(jnp.bfloat16)
    return np.concatenate(
        [np.concatenate([hi, hi], axis=1), np.concatenate([lo, np.zeros_like(lo)], axis=1)], axis=0
    )


def tap_values(distance):
    out = np.zeros(distance.shape, np.float32)
    for i, c in enumerate(TAPS):
        out[distance == i + 1] = c
    return out


def band(size, center):
    a = np.arange(size)
    distance = np.abs(a[:, None] - a[None, :])
    return np.where(distance == 0, np.float32(center), tap_values(distance))


def matrices(nx, ny):
    t_x = np.concatenate([band(nx, CENTER_X)] * 2, axis=1)
    t_y = np.zeros((2 * ny, 2 * ny), np.float32)
    t_y[:ny, :ny] = t_y[ny:, ny:] = band(ny, CENTER_Y)
    a, b = np.arange(ny)[:, None], np.arange(ny)[None, :]
    left = (a & 4) != 0
    place = np.where(left, (a & 3) - 4, ny + (a & 3))
    plane = np.where(left, (a + 4) % ny, a) >> 3
    target = np.where((b & 7) < 4, ny - 4 + (b & 7), (b & 7) - 4)
    onto = np.where(plane == b >> 3, tap_values(np.abs(place - target)), np.float32(0))
    return [jnp.asarray(m.astype(jnp.bfloat16)) for m in (t_x, t_y, onto)]


def shards(n_gx, n_gy, p_prev, p_cur, courant, snapshots, residual, rec_owner, rec_cell, signs):
    nz, nx, ny = p_cur.shape
    n = n_gx * n_gy
    recv_dev = rec_cell.shape[0]
    slots = -(-(2 * recv_dev // n) // 128) * 128
    chunks = nz // CHUNK
    anywhere = pl.BlockSpec(memory_space=pl.ANY)
    vmem = pl.BlockSpec(memory_space=pltpu.VMEM)
    dma = pltpu.SemaphoreType.DMA
    whole = jax.ShapeDtypeStruct(p_cur.shape, F32)
    mats = matrices(nx, ny)
    mat_scratch = [pltpu.VMEM(m.shape, BF16) for m in mats]
    table = jnp.asarray(step_table(NT, STEPS))
    state = (
        pltpu.VMEM((nz + 2 * HALO, nx, ny), F32),
        pltpu.VMEM((nz + 2 * HALO, nx, ny), F32),
        pltpu.VMEM((nz, nx, ny), F32),
        pltpu.VMEM((STEPS, nz, nx, ny), BF16),
        pltpu.VMEM((nz, nx, ny), F32),
        pltpu.VMEM((nx, ny), F32),
        pltpu.VMEM((CHUNK, 2 * HALO, ny), F32),
        pltpu.VMEM((nx, ny), F32),
    )
    held = pl.pallas_call(
        functools.partial(main_kernel, n_gx, n_gy),
        out_shape=state,
        in_specs=[pl.BlockSpec(memory_space=pltpu.SMEM)] + [anywhere] * 11,
        out_specs=(vmem,) * len(state),
        scratch_shapes=[
            pltpu.VMEM((1, recv_dev), I32),
            pltpu.VMEM((1, recv_dev), I32),
            pltpu.VMEM(table.shape, BF16),
            *mat_scratch,
            pltpu.VMEM(residual.shape, F32),
            pltpu.VMEM((STEPS, 2, nz, HALO, ny), F32),
            pltpu.VMEM((STEPS, 2, nz, HALO, ny), F32),
            pltpu.VMEM((STEPS, 2, chunks, nx // 2, ny), F32),
            pltpu.VMEM((STEPS, 2, chunks, nx // 2, ny), F32),
            pltpu.VMEM((nx, ny), F32),
            pltpu.VMEM((nx, 2 * STEPS * ny), F32),
            pltpu.VMEM((2, CHUNK // GROUP, nx, ny), F32),
            pltpu.VMEM((n, 8, slots), F32),
            pltpu.VMEM((n, 8, slots), F32),
            dma((11,)),
            dma((2 * STEPS * chunks,)),
            dma((2 * STEPS * chunks,)),
            dma((2 * STEPS * chunks,)),
            dma((2 * STEPS * chunks,)),
            dma((n,)),
            dma((n,)),
        ],
        compiler_params=pltpu.CompilerParams(
            collective_id=0, has_side_effects=True, vmem_limit_bytes=42 * 1024 * 1024
        ),
        name="adjoint_steps",
    )(
        signs,
        rec_owner.reshape(1, recv_dev),
        rec_cell.reshape(1, recv_dev),
        table,
        *mats,
        p_prev, p_cur, courant, snapshots, residual,
    )
    return pl.pallas_call(
        last_kernel,
        out_shape=(whole, whole),
        in_specs=[vmem] * len(state) + [anywhere] * 2,
        out_specs=(anywhere, anywhere),
        scratch_shapes=[
            *mat_scratch[:2],
            pltpu.VMEM((CHUNK, nx, ny), F32),
            pltpu.VMEM((CHUNK, nx, ny), F32),
            dma((2,)),
            dma((2 * chunks + 2 * (CHUNK // GROUP),)),
        ],
        compiler_params=pltpu.CompilerParams(vmem_limit_bytes=8 * 1024 * 1024),
        name="last_chunk",
    )(*held, *mats[:2])


def solution(mesh):
    placed = (
        P(None, "gx", "gy"),
        P(None, "gx", "gy"),
        P(None, "gx", "gy"),
        P(None, None, "gx", "gy"),
        P(None, ("gx", "gy"), None),
        P(("gx", "gy"), None),
        P(("gx", "gy")),
        P(),
    )
    return jax.shard_map(
        functools.partial(shards, mesh.shape["gx"], mesh.shape["gy"]),
        mesh=mesh,
        in_specs=placed,
        out_specs=(P(None, "gx", "gy"), P(None, "gx", "gy")),
        check_vma=False,
    )
```

```python
import functools
import math

import jax
import jax.numpy as jnp
import numpy as np
from jax import lax
from jax.experimental import pallas as pl
from jax.experimental.pallas import tpu as pltpu
from jax.sharding import PartitionSpec as P

STEPS = 3
NT = 128
RECV_DEPTH = 2
HALO = 4
CHUNK = 16
BLOCK = 256
GROUP = 8
SENDERS = 16

SCALE = 5040.0
CENTER_Y, CENTER_X = -43008.0, -42.0
TAPS = (8064.0, -1008.0, 128.0, -9.0)

F32 = jnp.float32
BF16 = jnp.bfloat16
I32 = jnp.int32
MESH = pl.DeviceIdType.MESH


def taps(distance):
    out = jnp.zeros(distance.shape, F32)
    for i, c in enumerate(TAPS):
        out = jnp.where(distance == i + 1, c, out)
    return out


def pieces(v):
    hi = v.astype(BF16)
    return hi, (v - hi.astype(F32)).astype(BF16)


def iota(shape, dim):
    return lax.broadcasted_iota(I32, shape, dim)


def lanes_dot(a, b, **kw):
    return lax.dot_general(a, b, (((1,), (1,)), ((), ())), preferred_element_type=F32, **kw)


def side_taps(nx):
    row = iota((16, 16), 0)
    src = iota((16, 16), 1) & 7
    place = jnp.where(src < 4, src - 4, nx + src - 4)
    target = jnp.where(row < 8, row, nx - 16 + row)
    return taps(jnp.abs(place - target)).astype(BF16)


def border_of(h_x, overs):
    cols = []
    for over in overs:
        hi, lo = pieces(over)
        cols.append(jnp.concatenate([hi.astype(F32), lo.astype(F32)], axis=0).astype(BF16))
    return jnp.dot(h_x, jnp.concatenate(cols, axis=1), preferred_element_type=F32)


def lateral(t_x, t_y, vs):
    (hi0, lo0), (hi1, lo1) = pieces(vs[0]), pieces(vs[1])
    hi = jnp.concatenate([hi0, hi1], axis=1)
    lo = jnp.concatenate([lo0, lo1], axis=1)
    return jnp.dot(
        jnp.concatenate([hi, lo, t_x[...]], axis=1),
        jnp.concatenate([t_y[...], t_y[...], hi, lo], axis=0),
        preferred_element_type=F32,
    )


def deep(cur, at):
    depth = TAPS[0] * (cur[at + 1] + cur[at - 1])
    for r in range(2, HALO + 1):
        depth = depth + TAPS[r - 1] * (cur[at + r] + cur[at - r])
    return depth


def with_border(lap, border):
    nx = lap.shape[0]
    return jnp.concatenate([lap[:8] + border[:8], lap[8 : nx - 8], lap[nx - 8 :] + border[8:]], axis=0)


def gather_edges(vs):
    lane = iota(vs[0].shape, 1)
    width = 1
    while len(vs) > 1:
        inside = (lane >= 8 * width - 4) & (lane < 16 * width - 4)
        vs = [
            jnp.where(inside, pltpu.roll(b, 8 * width, 1), a) for a, b in zip(vs[::2], vs[1::2])
        ]
        width *= 2
    return vs[0]


def to_sides(first, second):
    nx, ny = first.shape
    half = nx // 2
    lane = iota((nx, ny), 1)
    whole = jnp.where((lane >= ny // 2 - 4) & (lane < ny - 4), pltpu.roll(second, ny // 2, 1), first)
    top, low = whole[:half], pltpu.roll(whole[half:], 4, 1)
    odd = (iota((half, ny), 1) & 4) != 0
    return jnp.where(odd, top, low), jnp.where(odd, low, top)


def edge_terms(left, right, onto):
    half, ny = left.shape
    odd = (iota((half, ny), 1) & 4) != 0
    edges = jnp.concatenate(
        [jnp.where(odd, left, right), pltpu.roll(jnp.where(odd, right, left), ny - 4, 1)], axis=0
    )
    return jnp.dot(
        jnp.concatenate(pieces(edges), axis=1), jnp.concatenate([onto[...]] * 2, axis=0),
        preferred_element_type=F32,
    )


def placed_edge(terms, q):
    nx, ny = terms.shape
    lane = iota((nx, ny), 1)
    turned = pltpu.roll(terms, (2 * ny - 4 - 8 * q) & (ny - 1), 1)
    return jnp.where((lane < HALO) | (lane >= ny - HALO), turned, 0.0)


def main_kernel(
    n_gx, n_gy, signs, owner_h, cell_h, table_h, t_x_h, t_y_h, onto_h,
    p_prev, p_cur, courant_h, snaps_h, residual_h,
    buf_a, buf_b, courant, snaps, image, edge_out, over_out, source_out,
    owner, cell, table, t_x, t_y, onto, residual, sx, rx, sy, ry, edge, planes, packed,
    snd, got, load_sem, sxs, rxs, sys_, rys, snds, gots,
):
    n = n_gx * n_gy
    nz, nx, ny = p_cur.shape
    half, mid = nx // 2, ny // 2
    chunks = nz // CHUNK
    deeper = tuple(range(chunks - 1, 0, -1))
    gx, gy = lax.axis_index("gx"), lax.axis_index("gy")
    me = gx * n_gy + gy

    inner = pl.ds(HALO, nz)
    plan = [
        (p_cur, buf_a.at[inner]), (residual_h, residual), (owner_h, owner), (cell_h, cell), (table_h, table),
        (t_x_h, t_x), (t_y_h, t_y), (p_prev, buf_b.at[inner]), (courant_h, courant), (onto_h, onto),
        (snaps_h, snaps),
    ]
    loads = [pltpu.make_async_copy(s, d, load_sem.at[i]) for i, (s, d) in enumerate(plan)]
    for load in loads:
        load.start()

    barrier = pltpu.get_barrier_semaphore()

    def greet(o, carry):
        d = lax.rem(me + o, n)
        pl.semaphore_signal(
            barrier, inc=1, device_id=(d // n_gy, lax.rem(d, n_gy)), device_id_type=MESH
        )
        return carry

    lax.fori_loop(1, n, greet, 0)

    h_x = side_taps(nx)
    zero = jnp.zeros((HALO, nx, ny), F32)
    for buf in (buf_a, buf_b):
        buf[pl.ds(0, HALO)] = zero
        buf[pl.ds(HALO + nz, HALO)] = zero

    for side, absent in ((0, gx == 0), (1, gx == n_gx - 1)):

        @pl.when(absent)
        def _(side=side):
            for k in range(STEPS):
                rx[k, side] = jnp.zeros(rx.shape[2:], F32)

    for side, absent in ((0, gy == 0), (1, gy == n_gy - 1)):

        @pl.when(absent)
        def _(side=side):
            for k in range(STEPS):
                ry[k, side] = jnp.zeros(ry.shape[2:], F32)

    def pack(vs, k, g, j):
        for i, v in enumerate(vs):
            z = g * CHUNK + GROUP * j + i
            sx[k, 0, z] = v[nx - HALO :]
            sx[k, 1, z] = v[:HALO]
        packed[k % 2, j] = gather_edges(vs)

    def settle(k, g):
        sy[k, 0, g], sy[k, 1, g] = to_sides(packed[k % 2, 0], packed[k % 2, 1])

    def halo_copies(k, g):
        zs = pl.ds(g * CHUNK, CHUNK)
        out = []
        for side, step, send_ok, recv_ok in (
            (0, 1, gy < n_gy - 1, gy > 0),
            (1, -1, gy > 0, gy < n_gy - 1),
        ):
            i = (k * chunks + g) * 2 + side
            copy = pltpu.make_async_remote_copy(
                src_ref=sy.at[k, side, g], dst_ref=ry.at[k, side, g],
                send_sem=sys_.at[i], recv_sem=rys.at[i],
                device_id=(gx, lax.rem(gy + step + n_gy, n_gy)), device_id_type=MESH,
            )
            out.append((copy, send_ok, recv_ok))
        for side, step, send_ok, recv_ok in (
            (0, 1, gx < n_gx - 1, gx > 0),
            (1, -1, gx > 0, gx < n_gx - 1),
        ):
            i = (k * chunks + g) * 2 + side
            copy = pltpu.make_async_remote_copy(
                src_ref=sx.at[k, side, zs], dst_ref=rx.at[k, side, zs],
                send_sem=sxs.at[i], recv_sem=rxs.at[i],
                device_id=(lax.rem(gx + step + n_gx, n_gx), gy), device_id_type=MESH,
            )
            out.append((copy, send_ok, recv_ok))
        return out

    def send_halo(k, g, part=slice(0, 4)):
        for copy, send_ok, _ in halo_copies(k, g)[part]:
            pl.when(send_ok)(copy.start)

    def wait_halo(k, g):
        for copy, _, recv_ok in halo_copies(k, g):
            pl.when(recv_ok)(copy.wait_recv)

    def each(body):
        lax.fori_loop(0, CHUNK // GROUP, lambda j, c: (body(j), c)[1], 0)

    def beyond(k, z):
        return jnp.concatenate([rx[k, 0, z], rx[k, 1, z]], axis=0)

    loads[0].wait()
    for g in range(chunks):

        def first_pack(j, g=g):
            pack([buf_a[HALO + g * CHUNK + GROUP * j + i] for i in range(GROUP)], 0, g, j)

        each(first_pack)
        settle(0, g)

    pl.semaphore_wait(barrier, n - 1)
    for part in (slice(0, 2), slice(2, 4)):
        for g in deeper + (0,):
            send_halo(0, g, part)

    for load in loads[1:5]:
        load.wait()
    recv_dev = owner.shape[1]
    slots = snd.shape[2]
    upper = (iota((BLOCK, BLOCK), 0) < iota((BLOCK, BLOCK), 1)).astype(F32).astype(BF16)
    count = jnp.zeros((n, 1), F32)
    message = jnp.zeros((n * 8, slots), F32)
    part = iota((8, BLOCK), 0)
    shift = ny.bit_length() - 1
    for blk in range(recv_dev // BLOCK):
        rows = pl.ds(blk * BLOCK, BLOCK)
        enc = signs[0].astype(F32) * residual[0, rows, :]
        for s in range(1, residual.shape[0]):
            enc = enc + signs[s].astype(F32) * residual[s, rows, :]
        both = lanes_dot(table[...], jnp.concatenate(pieces(enc), axis=1))
        amps = both[:8] + both[8:]
        hi = amps.astype(BF16).astype(F32)
        c = cell[:, rows]
        at_x = (c >> shift).astype(F32)
        at_y = (c & (ny - 1)).astype(F32)
        payload = jnp.where((part & 1) == 0, hi, amps - hi)
        payload = jnp.where(part == 6, at_x, payload)
        payload = jnp.where(part == 7, at_y, payload)
        onehot = jnp.where(iota((n, BLOCK), 0) == owner[:, rows], 1.0, 0.0)
        before = jnp.dot(onehot.astype(BF16), upper, preferred_element_type=F32) + count
        count = count + jnp.sum(onehot, axis=1, keepdims=True)
        rank = jnp.sum(before * onehot, axis=0, keepdims=True)
        spread = (onehot[:, None, :] * payload[None]).reshape(n * 8, BLOCK).astype(BF16)
        slot = jnp.where(iota((slots, BLOCK), 0).astype(F32) == rank, 1.0, 0.0).astype(BF16)
        message = message + lanes_dot(spread, slot)
    snd[...] = message.reshape(n, 8, slots)
    got[me] = snd[me]

    def message_to(o):
        d = lax.rem(me + o, n)
        return pltpu.make_async_remote_copy(
            src_ref=snd.at[d], dst_ref=got.at[me], send_sem=snds.at[o], recv_sem=gots.at[o],
            device_id=(d // n_gy, lax.rem(d, n_gy)), device_id_type=MESH,
        )

    def post(o, carry):
        message_to(o).start()
        return carry

    def step_chunk(k, g, inside=False):
        cur, prev = (buf_a, buf_b) if k % 2 == 0 else (buf_b, buf_a)
        if not inside:
            wait_halo(k, g)
            edge[...] = edge_terms(ry[k, 0, g], ry[k, 1, g], onto)

        def body(j):
            qs = [GROUP * j + i for i in range(GROUP)]
            made = []
            for p in range(GROUP // 2):
                pair = qs[2 * p : 2 * p + 2]
                zs = [g * CHUNK + q for q in pair]
                vs = [cur[z + HALO] for z in zs]
                lap2 = lateral(t_x, t_y, vs)
                border2 = None if inside else border_of(h_x, [beyond(k, z) for z in zs])
                for i, (z, v) in enumerate(zip(zs, vs)):
                    cols = slice(i * ny, (i + 1) * ny)
                    lap = lap2[:, cols] + deep(cur, z + HALO)
                    if not inside:
                        lap = with_border(lap + placed_edge(edge[...], pair[i]), border2[:, cols])
                    if k == 0:
                        speed = courant[z] * (1.0 / SCALE)
                        courant[z] = speed
                    else:
                        speed = courant[z]
                    old = prev[z + HALO]
                    nxt = (2.0 * v - old) + speed * lap
                    if k == STEPS - 1:
                        image[z] = (
                            snaps[0, z].astype(F32) * old + snaps[1, z].astype(F32) * v
                            + snaps[2, z].astype(F32) * nxt
                        )
                    prev[z + HALO] = nxt
                    made.append(nxt)
            if k < STEPS - 1 and not inside:
                pack(made, k + 1, g, j)

        each(body)
        if k < STEPS - 1 and not inside and (k, g) != (0, 0):
            settle(k + 1, g)

    def complete(g):
        wait_halo(0, g)
        edge[...] = edge_terms(ry[0, 0, g], ry[0, 1, g], onto)

        def body(j):
            qs = [GROUP * j + i for i in range(GROUP)]
            made = []
            for p in range(GROUP // 2):
                zs = [g * CHUNK + q for q in qs[2 * p : 2 * p + 2]]
                border2 = border_of(h_x, [beyond(0, z) for z in zs])
                for i, z in enumerate(zs):
                    cols = slice(i * ny, (i + 1) * ny)
                    lap = with_border(placed_edge(edge[...], qs[2 * p + i]), border2[:, cols])
                    nxt = buf_b[z + HALO] + courant[z] * lap
                    buf_b[z + HALO] = nxt
                    made.append(nxt)
            pack(made, 1, g, j)

        each(body)
        if g:
            settle(1, g)
            send_halo(1, g)

    lax.fori_loop(1, n, post, 0)
    for load in loads[5:9]:
        load.wait()
    for g in deeper + (0,):
        step_chunk(0, g, inside=True)
    loads[9].wait()
    for g in deeper:
        complete(g)
    complete(0)

    def arrive(o, carry):
        d = lax.rem(me - o + n, n)
        pltpu.make_async_remote_copy(
            src_ref=snd.at[d], dst_ref=got.at[d], send_sem=snds.at[o], recv_sem=gots.at[o],
            device_id=(d // n_gy, lax.rem(d, n_gy)), device_id_type=MESH,
        ).wait_recv()
        return carry

    lax.fori_loop(1, n, arrive, 0)
    planes[...] = jnp.zeros(planes.shape, F32)
    row_x = iota((nx, slots), 0).astype(F32)
    row_y = iota((ny, slots), 0).astype(F32)

    def gather(j, carry):
        lhs, rhs = [], [[] for _ in range(2 * STEPS)]
        for i in range(SENDERS):
            block = got[SENDERS * j + i]
            lhs.append(jnp.where(row_x == block[6:7], 1.0, 0.0).astype(BF16))
            at_y = row_y == block[7:8]
            for h in range(2 * STEPS):
                rhs[h].append(jnp.where(at_y, block[h : h + 1], 0.0).astype(BF16))
        rhs = jnp.concatenate([jnp.concatenate(r, axis=1) for r in rhs], axis=0)
        planes[...] += lanes_dot(jnp.concatenate(lhs, axis=1), rhs)
        return carry

    lax.fori_loop(0, n // SENDERS, gather, 0)

    def source(k):
        cols = planes[:, 2 * k * ny : (2 * k + 2) * ny]
        return (SCALE * courant[RECV_DEPTH]) * (cols[:, :ny] + cols[:, ny:])

    at = HALO + RECV_DEPTH
    fixed = buf_b[at] + source(0)
    buf_b[at] = fixed
    sx[1, 0, RECV_DEPTH] = fixed[nx - HALO :]
    sx[1, 1, RECV_DEPTH] = fixed[:HALO]
    near = 8 * RECV_DEPTH - 4
    lane = iota((nx, ny), 1)
    packed[1, 0] = jnp.where(
        (lane >= near) & (lane < near + 8), pltpu.roll(fixed, 8 * RECV_DEPTH, 1), packed[1, 0]
    )
    settle(1, 0)
    send_halo(1, 0)
    for g in deeper:
        step_chunk(1, g)
        send_halo(2, g)
    buf_a[at] = buf_a[at] - source(1)
    step_chunk(1, 0)
    send_halo(2, 0)
    loads[10].wait()
    for g in deeper:
        step_chunk(2, g)
    source_out[...] = source(2)
    wait_halo(2, 0)
    edge_out[...] = edge_terms(ry[2, 0, 0], ry[2, 1, 0], onto)
    over_out[:, :HALO] = rx[2, 0, pl.ds(0, CHUNK)]
    over_out[:, HALO:] = rx[2, 1, pl.ds(0, CHUNK)]

    def finish(o, carry):
        message_to(o).wait_send()
        return carry

    lax.fori_loop(1, n, finish, 0)
    for k in range(STEPS):
        for g in range(chunks):
            for copy, send_ok, _ in halo_copies(k, g):
                pl.when(send_ok)(copy.wait_send)


def last_kernel(
    buf_a, buf_b, courant, snaps, image, edge, over, source, t_x_h, t_y_h,
    field_out, image_out,
    t_x, t_y, field0, image0, load_sem, out_sem,
):
    nz, nx, ny = courant.shape
    chunks = nz // CHUNK
    loads = [
        pltpu.make_async_copy(s, d, load_sem.at[i])
        for i, (s, d) in enumerate(((t_x_h, t_x), (t_y_h, t_y)))
    ]
    for load in loads:
        load.start()
    outs = []
    for g in range(chunks - 1, 0, -1):
        zs = pl.ds(g * CHUNK, CHUNK)
        outs += [
            pltpu.make_async_copy(
                buf_b.at[pl.ds(HALO + g * CHUNK, CHUNK)], field_out.at[zs], out_sem.at[2 * g]
            ),
            pltpu.make_async_copy(image.at[zs], image_out.at[zs], out_sem.at[2 * g + 1]),
        ]
    for out in outs:
        out.start()
    h_x = side_taps(nx)
    for load in loads:
        load.wait()

    def rest(j):
        zs = pl.ds(j * GROUP, GROUP)
        return [
            pltpu.make_async_copy(field0.at[zs], field_out.at[zs], out_sem.at[2 * chunks + 2 * j]),
            pltpu.make_async_copy(image0.at[zs], image_out.at[zs], out_sem.at[2 * chunks + 2 * j + 1]),
        ]

    def body(j, carry):
        for p in range(GROUP // 2):
            zs = [GROUP * j + 2 * p + i for i in range(2)]
            vs = [buf_a[z + HALO] for z in zs]
            lap2 = lateral(t_x, t_y, vs)
            border2 = border_of(h_x, [over[z] for z in zs])
            for i, (z, v) in enumerate(zip(zs, vs)):
                cols = slice(i * ny, (i + 1) * ny)
                lap = lap2[:, cols] + deep(buf_a, z + HALO) + placed_edge(edge[...], z)
                lap = with_border(lap, border2[:, cols])
                old = buf_b[z + HALO]
                nxt = (2.0 * v - old) + courant[z] * lap
                nxt = nxt + jnp.where(z == RECV_DEPTH, source[...], 0.0)
                field0[z] = nxt
                image0[z] = (
                    snaps[0, z].astype(F32) * old + snaps[1, z].astype(F32) * v
                    + snaps[2, z].astype(F32) * nxt
                )
        for out in rest(j):
            out.start()
        return carry

    lax.fori_loop(0, CHUNK // GROUP, body, 0)
    for j in range(CHUNK // GROUP):
        for out in rest(j):
            out.wait()
    for out in outs:
        out.wait()


def step_table(samples, steps):
    rows = np.arange(samples, dtype=np.float64)[None, :]
    cols = np.repeat(np.arange(steps, dtype=np.float64), 2)[:, None]
    table = np.cos(math.pi * (cols + 0.5) * (rows + 0.5) / samples) * math.sqrt(2.0 / samples)
    table = np.concatenate([table, np.zeros((8 - 2 * steps, samples))]).astype(np.float32)
    hi = table.astype(jnp.bfloat16)
    lo = (table - hi.astype(np.float32)).astype(jnp.bfloat16)
    return np.concatenate(
        [np.concatenate([hi, hi], axis=1), np.concatenate([lo, np.zeros_like(lo)], axis=1)], axis=0
    )


def tap_values(distance):
    out = np.zeros(distance.shape, np.float32)
    for i, c in enumerate(TAPS):
        out[distance == i + 1] = c
    return out


def band(size, center):
    a = np.arange(size)
    distance = np.abs(a[:, None] - a[None, :])
    return np.where(distance == 0, np.float32(center), tap_values(distance))


def matrices(nx, ny):
    t_x = np.concatenate([band(nx, CENTER_X)] * 2, axis=1)
    t_y = np.zeros((2 * ny, 2 * ny), np.float32)
    t_y[:ny, :ny] = t_y[ny:, ny:] = band(ny, CENTER_Y)
    a, b = np.arange(ny)[:, None], np.arange(ny)[None, :]
    left = (a & 4) != 0
    place = np.where(left, (a & 3) - 4, ny + (a & 3))
    plane = np.where(left, (a + 4) % ny, a) >> 3
    target = np.where((b & 7) < 4, ny - 4 + (b & 7), (b & 7) - 4)
    onto = np.where(plane == b >> 3, tap_values(np.abs(place - target)), np.float32(0))
    return [jnp.asarray(m.astype(jnp.bfloat16)) for m in (t_x, t_y, onto)]


def shards(n_gx, n_gy, p_prev, p_cur, courant, snapshots, residual, rec_owner, rec_cell, signs):
    nz, nx, ny = p_cur.shape
    n = n_gx * n_gy
    recv_dev = rec_cell.shape[0]
    slots = -(-(2 * recv_dev // n) // 128) * 128
    chunks = nz // CHUNK
    anywhere = pl.BlockSpec(memory_space=pl.ANY)
    vmem = pl.BlockSpec(memory_space=pltpu.VMEM)
    dma = pltpu.SemaphoreType.DMA
    whole = jax.ShapeDtypeStruct(p_cur.shape, F32)
    mats = matrices(nx, ny)
    mat_scratch = [pltpu.VMEM(m.shape, BF16) for m in mats]
    table = jnp.asarray(step_table(NT, STEPS))
    state = (
        pltpu.VMEM((nz + 2 * HALO, nx, ny), F32),
        pltpu.VMEM((nz + 2 * HALO, nx, ny), F32),
        pltpu.VMEM((nz, nx, ny), F32),
        pltpu.VMEM((STEPS, nz, nx, ny), BF16),
        pltpu.VMEM((nz, nx, ny), F32),
        pltpu.VMEM((nx, ny), F32),
        pltpu.VMEM((CHUNK, 2 * HALO, ny), F32),
        pltpu.VMEM((nx, ny), F32),
    )
    held = pl.pallas_call(
        functools.partial(main_kernel, n_gx, n_gy),
        out_shape=state,
        in_specs=[pl.BlockSpec(memory_space=pltpu.SMEM)] + [anywhere] * 11,
        out_specs=(vmem,) * len(state),
        scratch_shapes=[
            pltpu.VMEM((1, recv_dev), I32),
            pltpu.VMEM((1, recv_dev), I32),
            pltpu.VMEM(table.shape, BF16),
            *mat_scratch,
            pltpu.VMEM(residual.shape, F32),
            pltpu.VMEM((STEPS, 2, nz, HALO, ny), F32),
            pltpu.VMEM((STEPS, 2, nz, HALO, ny), F32),
            pltpu.VMEM((STEPS, 2, chunks, nx // 2, ny), F32),
            pltpu.VMEM((STEPS, 2, chunks, nx // 2, ny), F32),
            pltpu.VMEM((nx, ny), F32),
            pltpu.VMEM((nx, 2 * STEPS * ny), F32),
            pltpu.VMEM((2, CHUNK // GROUP, nx, ny), F32),
            pltpu.VMEM((n, 8, slots), F32),
            pltpu.VMEM((n, 8, slots), F32),
            dma((11,)),
            dma((2 * STEPS * chunks,)),
            dma((2 * STEPS * chunks,)),
            dma((2 * STEPS * chunks,)),
            dma((2 * STEPS * chunks,)),
            dma((n,)),
            dma((n,)),
        ],
        compiler_params=pltpu.CompilerParams(
            collective_id=0, has_side_effects=True, vmem_limit_bytes=42 * 1024 * 1024
        ),
        name="adjoint_steps",
    )(
        signs,
        rec_owner.reshape(1, recv_dev),
        rec_cell.reshape(1, recv_dev),
        table,
        *mats,
        p_prev, p_cur, courant, snapshots, residual,
    )
    return pl.pallas_call(
        last_kernel,
        out_shape=(whole, whole),
        in_specs=[vmem] * len(state) + [anywhere] * 2,
        out_specs=(anywhere, anywhere),
        scratch_shapes=[
            *mat_scratch[:2],
            pltpu.VMEM((CHUNK, nx, ny), F32),
            pltpu.VMEM((CHUNK, nx, ny), F32),
            dma((2,)),
            dma((2 * chunks + 2 * (CHUNK // GROUP),)),
        ],
        compiler_params=pltpu.CompilerParams(vmem_limit_bytes=8 * 1024 * 1024),
        name="last_chunk",
    )(*held, *mats[:2])


def solution(mesh):
    placed = (
        P(None, "gx", "gy"),
        P(None, "gx", "gy"),
        P(None, "gx", "gy"),
        P(None, None, "gx", "gy"),
        P(None, ("gx", "gy"), None),
        P(("gx", "gy"), None),
        P(("gx", "gy")),
        P(),
    )
    return jax.shard_map(
        functools.partial(shards, mesh.shape["gx"], mesh.shape["gy"]),
        mesh=mesh,
        in_specs=placed,
        out_specs=(P(None, "gx", "gy"), P(None, "gx", "gy")),
        check_vma=False,
    )
```
